32 devices in a mesh: frames: 4 (over y, core), win: 8 (over z, x).
Axes of the slice: x: 2, y: 2, z: 4, core: 2. Of those that a mesh axis runs over, the one named last changes fastest.
Arguments:
- memberships: float32 [8, 256, 4096], P('win', 'frames'), as said below
- lag_times: int32 [8], P('win'), may hold values from 1 to 8, as said below
- segment_ids: int32 [8, 256], P('win'), may hold values from 0 to 7, never falling along the last dimension, each value on 1 to 128 neighbouring positions
- bias_codes: int32 [8, 4096], P('win'), may hold values from 0 to 511
Outputs:
- free_energy: float32 [4096], P('frames')
- log_multipliers: float32 [8, 4096], P('win', 'frames')
The draws below stay inside these ranges and needn't reach their ends.
Inputs may be any that keep to these rules, and one draw needn't show every extreme that they name: Positive; each frame's memberships sum to one up to rounding. `lag_times`: some window's lag time is 8.
All inputs are finite; a program needn't handle non-finite values.
Results may differ from the reference program's by a relative error of at most 0.00041.
Values may be sent and summed in bfloat16 or wider, within the bound.
No kernel may reach another device: no remote copies, remote signals or barrier semaphores. Data moves between devices by JAX's collectives and lax.ppermute only.
A program may use at most 64 MiB of HBM per device.

```python
import math
import jax
import jax.numpy as jnp
import numpy as np
from jax import lax

STATES = 4096
TOK_DEV = 64
LAGMAX = 8
ITERS = 2
WINDOWS = 8
TOKENS = 256
N_FRAMES = 4


def draw_memberships(key, part):
    key_list = jax.random.split(jax.random.fold_in(key, 11), 4)
    latent_dims = 16
    centres = jax.random.normal(key_list[0], (latent_dims, STATES), jnp.float32)
    centres = centres / jnp.sqrt(jnp.sum(centres * centres, axis=0, keepdims=True))
    anchor = jax.random.normal(key_list[1], (WINDOWS, 1, latent_dims), jnp.float32)
    fresh = jax.random.normal(key_list[2], (WINDOWS, TOKENS + 2, latent_dims), jnp.float32)
    moving = (fresh[:, 2:] + fresh[:, 1:-1] + fresh[:, :-2]) * (1.0 / jnp.sqrt(3.0))
    latent_path = 0.7 * anchor + moving
    latent_path = latent_path / jnp.sqrt(jnp.sum(latent_path * latent_path, axis=-1, keepdims=True))
    sharpness = 8.0
    jitter = jax.random.normal(key_list[3], (WINDOWS, TOKENS, STATES), jnp.float32)
    logits = sharpness * jnp.einsum('wtd,ds->wts', latent_path, centres)
    spread = jax.nn.softmax(logits + jitter, axis=-1)
    return 0.98 * spread + 0.02 / STATES


def draw_lag_times(key, part):
    key_list = jax.random.split(jax.random.fold_in(key, 23), 2)
    values = jax.random.randint(key_list[0], (WINDOWS,), 1, LAGMAX + 1)
    chosen = jax.random.randint(key_list[1], (), 0, WINDOWS)
    return jnp.where(jnp.arange(WINDOWS) == chosen, LAGMAX, values).astype(jnp.int32)


def place_ends(drawn, stream_key, smallest, top_value):
    longest = drawn.shape.index(max(drawn.shape))
    spots = []
    for shift in (0, 1):
        where = [jax.random.randint(jax.random.fold_in(stream_key, axis), (), 0, length) for axis, length in enumerate(drawn.shape)]
        where[longest] = (where[longest] + shift) % drawn.shape[longest]
        spots.append(tuple(where))
    return drawn.at[spots[0]].set(smallest).at[spots[1]].set(top_value)


def split_up(amount, total, limit, lean):
    weights = [(1 << 20) // math.isqrt(grade ** lean) + 1 for grade in range(2, amount + 1)]
    surplus, holding = total - limit - (amount - 1), [1] * (amount - 1)
    while surplus > 0:
        movable = [i for i in range(amount - 1) if holding[i] < limit]
        pool, remaining = sum([weights[i] for i in movable]), surplus
        for i in movable:
            extra = min(limit - holding[i], max(1, remaining * weights[i] // pool), surplus)
            holding[i] = holding[i] + extra
            surplus = surplus - extra
    return np.array([limit] + holding)


def ragged_sizes(own_key, count, total, most, skew):
    if count == 2:
        one = jax.random.randint(own_key, (), max(1, total - most), min(most, total - 1) + 1)
        return jnp.stack([one, total - one])
    lengths = jnp.asarray(split_up(count, total, most, skew), jnp.int32)
    couples = (count - 1) // 2
    donor, receiver = lengths[1:1 + 2 * couples:2], lengths[2:2 + 2 * couples:2]
    room = jnp.minimum(donor - 1, most - receiver)
    passed = jax.random.randint(jax.random.fold_in(own_key, 1), (couples,), 0, 1 << 20) % (room + 1)
    lengths = lengths.at[1:1 + 2 * couples:2].set(donor - passed).at[2:2 + 2 * couples:2].set(receiver + passed)
    return lengths[jax.random.permutation(jax.random.fold_in(own_key, 2), count)]


def setup_inputs(seed: int = 0) -> dict:
    key_of = jax.random.split(jax.random.key(seed), 5)
    return {
        "memberships": draw_memberships(jax.random.fold_in(key_of[4], 71), 0),
        "lag_times": draw_lag_times(jax.random.fold_in(key_of[4], 71), 0),
        "segment_ids": jax.vmap(lambda own: jnp.searchsorted(jnp.cumsum(ragged_sizes(own, 2 * N_FRAMES, TOKENS, 2 * TOK_DEV, 1)), jnp.arange(TOKENS), side="right"))(jax.random.split(key_of[2], WINDOWS)).reshape((WINDOWS, TOKENS)).astype(jnp.int32),
        "bias_codes": place_ends(jax.random.randint(key_of[3], (WINDOWS, STATES), 0, 512), jax.random.fold_in(key_of[3], 1), 0, 511).astype(jnp.int32),
    }


bias_unit = 1.0 / 128.0


def window_counts(member, lag_time, segment_row):
    frames_all = member.shape[0]
    states = member.shape[1]
    padding = jnp.zeros((LAGMAX, states), member.dtype)
    extended = jnp.concatenate([member, padding], axis=0)
    shifted = lax.dynamic_slice_in_dim(extended, lag_time.astype(jnp.int32), frames_all, 0)
    segment_ext = jnp.concatenate([segment_row, jnp.full((LAGMAX,), -1, jnp.int32)])
    segment_later = lax.dynamic_slice_in_dim(segment_ext, lag_time.astype(jnp.int32), frames_all, 0)
    later = jnp.where((segment_row == segment_later)[:, None], shifted, jnp.zeros((), member.dtype))
    counts = jnp.dot(member.T, later, preferred_element_type=jnp.float32)
    return counts + counts.T


def reference(memberships, lag_times, segment_ids, bias_codes):
    member = memberships.astype(jnp.bfloat16)
    sym_counts = lax.map(lambda packed: window_counts(packed[0], packed[1], packed[2]), (member, lag_times, segment_ids))
    gammas = jnp.exp(-bias_codes.astype(jnp.float32) * bias_unit)
    multipliers = jnp.sum(sym_counts, axis=2) * 0.5
    state_counts = jnp.sum(multipliers, axis=0)
    window_totals = jnp.sum(multipliers, axis=1)
    weights = jnp.full((STATES,), 1.0 / STATES, jnp.float32)
    for sweep in range(ITERS):
        def one_window(packed):
            counts, gamma_row, mult_row = packed
            scaled = gamma_row * weights
            denom = mult_row[:, None] * scaled[None, :] + scaled[:, None] * mult_row[None, :]
            ratios = counts / denom
            new_mult = mult_row * jnp.sum(ratios * scaled[None, :], axis=1)
            terms = gamma_row * jnp.sum(ratios * mult_row[None, :], axis=1)
            return new_mult, terms

        new_mults, terms = lax.map(one_window, (sym_counts, gammas, multipliers))
        raw = state_counts / jnp.sum(terms, axis=0)
        weights = raw / jnp.sum(raw)
        multipliers = new_mults
    free_energy = -jnp.log(STATES * weights)
    log_multipliers = jnp.log(multipliers * STATES / window_totals[:, None])
    return free_energy, log_multipliers
```

```python
import jax
import jax.numpy as jnp
from jax import lax
from jax.experimental import pallas as pl
from jax.experimental.pallas import tpu as pltpu
from jax.sharding import PartitionSpec as P

ITERS = 2
LANES = 128

bias_unit = 1.0 / 128.0


def split3(x):
    high = x.astype(jnp.bfloat16)
    rest = x - high.astype(jnp.float32)
    middle = rest.astype(jnp.bfloat16)
    low = (rest - middle.astype(jnp.float32)).astype(jnp.bfloat16)
    return jnp.concatenate([high, middle, low], axis=0)


def exact_dot(x, matrix):
    out = jnp.dot(split3(x), matrix, preferred_element_type=jnp.float32)
    number = x.shape[0]
    return (out[:number] + out[number : 2 * number]) + out[2 * number :]


def column_of(row):
    rows = row.shape[1]
    return jnp.transpose(jnp.broadcast_to(row, (LANES, rows)))


def row_of(partial):
    return jnp.sum(jnp.transpose(partial), axis=0, keepdims=True)


def column_tile(states):
    for width in (512, 256, 128):
        if states % width == 0:
            return width
    return states


def add_tile(counts, ratio_col, ratio_row, plain_ref, scaled_ref):
    rows, width = counts.shape
    plain = plain_ref[...]
    scaled = scaled_ref[...]
    for lane in range(0, width, LANES):
        r_row = ratio_row[:, lane : lane + LANES]
        part = counts[:, lane : lane + LANES] / (ratio_col + r_row)
        plain = plain + part
        scaled = scaled + part * r_row
    plain_ref[...] = plain
    scaled_ref[...] = scaled


def first_kernel(where, moved, joined, codes, *refs):
    blocks = refs[:-11]
    counts_out, mult_out, terms_out, ratio_out = refs[-11:-7]
    pair, left, ratio_row, ratio_col, plain, scaled, sem = refs[-7:]
    frames_all, states = moved.shape[0], pair.shape[1]
    rows = left.shape[0]
    frames_dev = blocks[0].shape[0]
    copies = [
        pltpu.make_async_copy(
            block, pair.at[pl.ds(frames_all + i * frames_dev, frames_dev), :], sem.at[i]
        )
        for i, block in enumerate(blocks)
    ]
    for copy in copies:
        copy.start()
    for copy in copies:
        copy.wait()
    first = pl.multiple_of(where[0] * rows, LANES)
    member = pair[pl.ds(frames_all, frames_all), :]
    ones = jnp.ones((8, states), jnp.bfloat16)
    sums = lax.dot_general(ones, member, (((1,), (1,)), ((), ())), preferred_element_type=jnp.float32)
    near = exact_dot(sums, joined[...])
    mult = exact_dot(near, member)[:1] * 0.5
    gammas = jnp.exp(codes[...].astype(jnp.float32) * -bias_unit)
    mult_out[...] = mult
    ratio_row[...] = gammas * (1.0 / states) / mult
    pair[pl.ds(0, frames_all), :] = jnp.dot(
        moved[...], member, preferred_element_type=jnp.float32
    ).astype(jnp.bfloat16)
    own = pl.ds(first, rows)
    left[:, :frames_all] = jnp.transpose(pair[pl.ds(frames_all, frames_all), own])
    left[:, frames_all:] = jnp.transpose(pair[pl.ds(0, frames_all), own])
    ratio_col[...] = column_of(ratio_row[:, own])
    plain[...] = jnp.zeros_like(plain)
    scaled[...] = jnp.zeros_like(scaled)
    width = column_tile(states)

    @pl.loop(0, states // width)
    def _(step):
        columns = pl.ds(pl.multiple_of(step * width, width), width)
        tile = jnp.dot(left[...], pair[:, columns], preferred_element_type=jnp.float32)
        counts_out[:, columns] = tile
        add_tile(tile, ratio_col[...], ratio_row[:, columns], plain, scaled)

    gamma_own = jnp.exp(codes[:, own].astype(jnp.float32) * -bias_unit)
    terms = gamma_own / mult_out[:, own] * row_of(plain[...])
    terms_out[...] = terms
    ratio_out[...] = row_of(scaled[...]) * states / terms


def second_kernel(where, given, mult, codes, counts, terms_out, logs_out, state_counts, new_mult, ratio_row, ratio_col, plain, scaled):
    rows = terms_out.shape[1]
    states = codes.shape[1]
    number = given.shape[0] // (states // rows)
    own_window = lax.broadcasted_iota(jnp.int32, (number, rows), 0) == where[1]
    gammas = jnp.exp(codes[...].astype(jnp.float32) * -bias_unit)
    for block in range(states // rows):
        here = slice(block * rows, (block + 1) * rows)
        mults = given[block * number : (block + 1) * number, :rows]
        others = given[block * number : (block + 1) * number, rows:]
        part = 2.0 * mults / (1.0 + others)
        terms = jnp.where(own_window, part * states, others)
        new_mult[:, here] = jnp.sum(jnp.where(own_window, part * others, 0.0), axis=0, keepdims=True)
        total = jnp.sum(mults, axis=0, keepdims=True)
        state_counts[:, here] = total
        ratio_row[:, here] = total / jnp.sum(terms, axis=0, keepdims=True)
    raw = ratio_row[...]
    weights = raw / jnp.sum(raw)
    ratio_row[...] = gammas * weights / new_mult[...]
    own = pl.ds(pl.multiple_of(where[0] * rows, LANES), rows)
    ratio_col[...] = column_of(ratio_row[:, own])
    plain[...] = jnp.zeros_like(plain)
    scaled[...] = jnp.zeros_like(scaled)
    width = column_tile(states)

    @pl.loop(0, states // width)
    def _(step):
        columns = pl.ds(pl.multiple_of(step * width, width), width)
        add_tile(counts[:, columns], ratio_col[...], ratio_row[:, columns], plain, scaled)

    gamma_own = jnp.exp(codes[:, own].astype(jnp.float32) * -bias_unit)
    terms_out[...] = gamma_own / new_mult[:, own] * row_of(plain[...])
    window_total = jnp.sum(mult[...])
    logs_out[...] = jnp.log(row_of(scaled[...]) * states / window_total)


def last_kernel(where, given, state_counts, energy_out, raw_row):
    rows = energy_out.shape[1]
    states = state_counts.shape[1]
    number = given.shape[0] // (states // rows)
    for block in range(states // rows):
        here = slice(block * rows, (block + 1) * rows)
        terms = jnp.sum(given[block * number : (block + 1) * number, :], axis=0, keepdims=True)
        raw_row[:, here] = state_counts[:, here] / terms
    own = pl.ds(pl.multiple_of(where[0] * rows, LANES), rows)
    total = jnp.sum(raw_row[...])
    energy_out[...] = -jnp.log(raw_row[:, own] / total * states)


def vector(width, dtype=jnp.float32):
    return jax.ShapeDtypeStruct((1, width), dtype)


def scratch(*shape, dtype=jnp.float32):
    return pltpu.VMEM(shape, dtype)


def everyone(block):
    return lax.all_to_all(block, ("frames", "win"), 0, 0, tiled=True)


def shards(memberships, lag_times, segment_ids, bias_codes):
    member = memberships[0].astype(jnp.bfloat16)
    frames_dev, states = member.shape
    frames_all = segment_ids.shape[1]
    number = lax.axis_size("frames")
    windows = lax.axis_size("win")
    rows = states // number
    position = lax.axis_index("frames")
    window = lax.axis_index("win")
    lag_time = lag_times[0]
    partner = [(i, i ^ 1) for i in range(number)]
    blocks = []
    order = []
    for step in range(0, number, 2):
        if step == 0:
            near = member
        else:
            near = lax.ppermute(member, "frames", [((i + step) % number, i) for i in range(number)])
        blocks.append(near)
        order.append((position + step) % number)
    for step in range(number // 2):
        blocks.insert(2 * step + 1, lax.ppermute(blocks[2 * step], "frames", partner))
        order.insert(2 * step + 1, order[2 * step] ^ 1)
    places = jnp.concatenate([block * frames_dev + jnp.arange(frames_dev) for block in order])
    segments = jnp.concatenate(
        [lax.dynamic_slice_in_dim(segment_ids[0], block * frames_dev, frames_dev, 0) for block in order]
    )
    same = segments[:, None] == segments[None, :]
    ahead = same & (places[None, :] == places[:, None] + lag_time)
    behind = same & (places[None, :] + lag_time == places[:, None])
    moved = ahead.astype(jnp.bfloat16)
    joined = (ahead | behind).astype(jnp.bfloat16)
    where = jnp.stack([position, window]).astype(jnp.int32)
    smem = pl.BlockSpec(memory_space=pltpu.SMEM)
    vmem = pl.BlockSpec(memory_space=pltpu.VMEM)
    hbm = pl.BlockSpec(memory_space=pl.ANY)
    sums = [scratch(1, states), scratch(rows, LANES), scratch(rows, LANES), scratch(rows, LANES)]
    counts, mult, terms, odds = pl.pallas_call(
        first_kernel,
        out_shape=(
            COUNTS((rows, states), jnp.float32),
            vector(states),
            vector(rows),
            vector(rows),
        ),
        in_specs=[smem, vmem, vmem, vmem] + [hbm] * number,
        out_specs=(vmem,) * 4,
        scratch_shapes=[
            scratch(2 * frames_all, states, dtype=jnp.bfloat16),
            scratch(rows, 2 * frames_all, dtype=jnp.bfloat16),
        ]
        + sums
        + [pltpu.SemaphoreType.DMA((number,))],
        compiler_params=pltpu.CompilerParams(vmem_limit_bytes=40 << 20),
        name="first",
    )(where, moved, joined, bias_codes, *blocks)
    mult_rows = lax.dynamic_slice_in_dim(mult, position * rows, rows, 1)
    target = lax.broadcasted_iota(jnp.int32, (number * windows, 1), 0) % windows
    sent = jnp.where(target == window, odds, terms)
    sent = jnp.concatenate([jnp.broadcast_to(mult_rows, sent.shape), sent], axis=1)
    given = everyone(sent)
    terms, logs, state_counts = pl.pallas_call(
        second_kernel,
        out_shape=(vector(rows), vector(rows), vector(states)),
        in_specs=[smem, vmem, vmem, vmem, vmem],
        out_specs=(vmem,) * 3,
        scratch_shapes=[scratch(1, states)] + sums,
        compiler_params=pltpu.CompilerParams(vmem_limit_bytes=40 << 20),
        name="second",
    )(where, given, mult, bias_codes, counts)
    given = everyone(jnp.broadcast_to(terms, (number * windows, rows)))
    energy = pl.pallas_call(
        last_kernel,
        out_shape=vector(rows),
        in_specs=[smem, vmem, vmem],
        out_specs=vmem,
        scratch_shapes=[scratch(1, states)],
        name="last",
    )(where, given, state_counts)
    return energy[0], logs


COUNTS = jax.ShapeDtypeStruct


def solution(mesh):
    placed = (P("win", "frames", None), P("win"), P("win", None), P("win", None))
    return jax.shard_map(
        shards,
        mesh=mesh,
        in_specs=placed,
        out_specs=(P("frames"), P("win", "frames")),
        check_vma=False,
    )
```

```python
import math

import jax
import jax.numpy as jnp
from jax import lax
from jax.experimental import pallas as pl
from jax.experimental.pallas import tpu as pltpu
from jax.sharding import PartitionSpec as P


LANES = 128
PIECES = 4

bias_unit = 1.0 / 128.0


def chunk_bounds(states, group):
    return [(0, group), (group, states)] if states > group else [(0, states)]


def granule(states, group):
    size = group
    for low, high in chunk_bounds(states, group):
        size = math.gcd(size, high - low)
    return size


def wrapped(place, states):
    return jnp.where(place >= states, place - states, place)


def split3(x):
    high = x.astype(jnp.bfloat16)
    rest = x - high.astype(jnp.float32)
    middle = rest.astype(jnp.bfloat16)
    low = (rest - middle.astype(jnp.float32)).astype(jnp.bfloat16)
    return high, middle, low


def gamma_of(codes):
    return jnp.exp(codes.astype(jnp.float32) * -bias_unit)


def spread(folded, column_ref):
    for i in range(folded.shape[0]):
        square = jnp.broadcast_to(folded[i : i + 1, :], (LANES, LANES))
        column_ref[i * LANES : (i + 1) * LANES, :] = jnp.transpose(square)


def gathered(partial_ref):
    rows = partial_ref.shape[0]
    return jnp.concatenate(
        [
            jnp.sum(jnp.transpose(partial_ref[i : i + LANES, :]), axis=0, keepdims=True)
            for i in range(0, rows, LANES)
        ],
        axis=0,
    )


def column_tile(width):
    for tile in (512, 256, 128):
        if width % tile == 0:
            return tile


def add_tile(counts, ratio_col, ratio_rows, plain_ref, scaled_ref):
    plain = plain_ref[...]
    scaled = scaled_ref[...]
    for i, r_row in enumerate(ratio_rows):
        part = counts[:, i * LANES : (i + 1) * LANES] / (ratio_col + r_row)
        plain = plain + part
        scaled = scaled + part * r_row
    plain_ref[...] = plain
    scaled_ref[...] = scaled


def place():
    position = lax.axis_index("frames")
    return position, lax.axis_index("win"), position % 2, position // 2


def fetched(sources, targets, sem):
    copies = [pltpu.make_async_copy(a, b, sem.at[i]) for i, (a, b) in enumerate(zip(sources, targets))]
    for copy in copies:
        copy.start()
    for copy in copies:
        copy.wait()


def prepare_kernel(group, given, *outs):
    member, sem = outs[-2:]
    whole, parts = outs[0], outs[1:-2]
    height = given.shape[1] // PIECES
    pieces = [pl.ds(i * height, height) for i in range(PIECES)]
    fetched([given.at[:, piece, :] for piece in pieces], [member.at[:, piece, :] for piece in pieces], sem)
    frames_dev, states = member.shape[1:]
    bounds = chunk_bounds(states, group)
    size = granule(states, group)
    own_chip = place()[3]
    total = jnp.zeros((frames_dev, LANES), jnp.float32)
    for j in range(0, states, size):
        source = pl.multiple_of(wrapped(own_chip * group + j, states), size)
        block = member[0, :, pl.ds(source, size)].astype(jnp.bfloat16)
        whole[:, j : j + size] = block
        wide = block.astype(jnp.float32)
        for i in range(0, size, LANES):
            total = total + wide[:, i : i + LANES]
    sums = jnp.broadcast_to(jnp.sum(total, axis=1, keepdims=True), (frames_dev, LANES))
    high, middle, low = split3(sums)
    lane = lax.broadcasted_iota(jnp.int32, sums.shape, 1)
    none = jnp.zeros_like(sums)
    packed = jnp.where(lane == 0, high.astype(jnp.float32), none)
    packed = jnp.where(lane == 1, middle.astype(jnp.float32), packed)
    packed = jnp.where(lane == 2, low.astype(jnp.float32), packed).astype(jnp.bfloat16)
    whole[:, states:] = packed
    for chip in range(1, states // group):
        base = (own_chip - chip) * group
        base = jnp.where(base < 0, base + states, base)
        for c, (low_end, high_end) in enumerate(bounds):
            part = parts[(chip - 1) * len(bounds) + c]
            for j in range(low_end, high_end, size):
                source = pl.multiple_of(wrapped(base + j, states), size)
                part[:, j - low_end : j - low_end + size] = member[0, :, pl.ds(source, size)].astype(jnp.bfloat16)
            if c == 0:
                part[:, high_end:] = packed


def plan_kernel(number, group, lag, segments_in, codes_in, inner, outer, joined, gammas, segments, codes, sem):
    fetched([segments_in, codes_in], [segments, codes], sem)
    frames_all = segments.shape[1]
    frames_dev = frames_all // number
    near = 2 * frames_dev
    _, _, core, own_chip = place()
    lag_time = lag[0]
    grid = (frames_all, frames_all)
    row = lax.broadcasted_iota(jnp.int32, grid, 0)
    frame = row
    for i in range(number):
        owner = lax.rem(own_chip + i // 2, number // 2) * 2 + (core if i % 2 == 0 else 1 - core)
        inside = (row >= i * frames_dev) & (row < (i + 1) * frames_dev)
        frame = jnp.where(inside, row + (owner - i) * frames_dev, frame)
    frame = frame.astype(jnp.float32)
    seg_row = jnp.broadcast_to(segments[...].astype(jnp.float32), grid)
    col = lax.broadcasted_iota(jnp.int32, grid, 1).astype(jnp.float32)
    seg = jnp.sum(jnp.where(frame == col, seg_row, 0.0), axis=1, keepdims=True)
    seg_from = jnp.broadcast_to(seg, grid)
    seg_to = jnp.transpose(seg_from)
    frame_to = jnp.transpose(frame)
    ahead = frame_to - frame
    same = seg_from == seg_to
    lag_float = lag_time.astype(jnp.float32)
    forward = same & (ahead == lag_float)
    backward = same & (ahead == -lag_float)
    joined[...] = jnp.where(forward | backward, 1.0, 0.0).astype(jnp.bfloat16)
    forward = jnp.where(forward, 1.0, 0.0)
    inner[...] = forward[:near, :near].astype(jnp.bfloat16)
    if number > 2:
        below = frame < (own_chip * near).astype(jnp.float32)
        touching = jnp.where(below, forward, jnp.where(backward, 1.0, 0.0))
        outer[...] = touching[near:, :].astype(jnp.bfloat16)
    size = granule(codes.shape[0] * LANES, group) // LANES
    for i in range(0, codes.shape[0], size):
        start = wrapped(own_chip * (group // LANES) + i, codes.shape[0])
        gammas[i : i + size, :] = gamma_of(codes[pl.ds(pl.multiple_of(start, size), size), :])


def near_kernel(bounds, whole, beside, inner, *refs):
    counts = refs[: len(bounds)]
    pair, left = refs[len(bounds) :]
    frames_dev = whole.shape[0]
    near = 2 * frames_dev
    rows = left.shape[0]
    states = pair.shape[1]
    own = pl.ds(pl.multiple_of(place()[2] * rows, rows), rows)
    pair[near : near + frames_dev, :] = whole[:, :states]
    pair[near + frames_dev :, :] = beside[:, :states]
    pair[:near, :] = jnp.dot(inner[...], pair[near:, :], preferred_element_type=jnp.float32).astype(jnp.bfloat16)
    left[:, :near] = jnp.transpose(pair[near:, own])
    left[:, near:] = jnp.transpose(pair[:near, own])
    for (low_end, high_end), count in zip(bounds, counts):
        tile = column_tile(high_end - low_end)

        @pl.loop(0, (high_end - low_end) // tile)
        def _(step):
            here = pl.ds(pl.multiple_of(step * tile, tile), tile)
            there = pl.ds(pl.multiple_of(low_end + step * tile, tile), tile)
            count[:, here] = jnp.dot(left[...], pair[:, there], preferred_element_type=jnp.float32)


def counts_kernel(bounds, which, number, *refs):
    low_end, high_end = bounds[which]
    width = high_end - low_end
    is_first, is_last = which == 0, which == len(bounds) - 1
    refs = list(refs)
    take = lambda k: [refs.pop(0) for _ in range(k)]
    gammas, counts_in = take(2)
    blocks = take(number)
    far = number > 2
    if is_first:
        outer, joined = take(2) if far else take(1) * 2
    else:
        plain_in, scaled_in, column, left, outer, mult_own_ref = take(6)
    counts_out, mult_out = take(2)
    if not is_last:
        plain, scaled = take(2)
    if is_first and not is_last:
        column, left, steps = take(3)
        mult_own_ref = mult_out
    if is_last:
        (sent,) = take(1)
        plain, scaled = take(2)
    if is_first and is_last:
        column, left, steps = take(3)
        mult_own_ref = mult_out
    pair, ratio = take(2)
    frames_dev = blocks[0].shape[0]
    frames_all = number * frames_dev
    away = frames_all - 2 * frames_dev
    rows = plain.shape[0]
    states = gammas.shape[0] * LANES
    depth = rows // LANES
    _, window, core, _ = place()
    own_rows = pl.ds(pl.multiple_of(core * depth, depth), depth)
    tile = column_tile(width)
    if is_first:
        sums = [block[:, states:] for block in blocks[:2]] + [block[:, width:] for block in blocks[2:]]
        column_sums = jnp.dot(joined[...], jnp.concatenate(sums, axis=0), preferred_element_type=jnp.float32)
        turned = jnp.transpose(column_sums)
        line = turned[0:1] + turned[1:2] + turned[2:3]
        parts = [jnp.broadcast_to(part.astype(jnp.float32), (16, frames_all)).astype(jnp.bfloat16) for part in split3(line)]
        steps[:48, :] = jnp.concatenate(parts, axis=0)
        if away:
            steps[48:, :] = outer[...]
        step_matrix = steps
    else:
        step_matrix = outer
    for j in range(0, width, tile):
        local = [block[:, low_end + j : low_end + j + tile] for block in blocks[:2]]
        others = [block[:, j : j + tile] for block in blocks[2:]]
        member = jnp.concatenate(local + others, axis=0)
        product = jnp.dot(step_matrix[...], member, preferred_element_type=jnp.float32)
        mult_row = (product[0:1] + product[16:17] + product[32:33]) * 0.5
        for i in range(tile // LANES):
            mult_out[j // LANES + i : j // LANES + i + 1, :] = mult_row[:, i * LANES : (i + 1) * LANES]
        if away:
            pair[:away, j : j + tile] = product[48:].astype(jnp.bfloat16)
            pair[away:, j : j + tile] = jnp.concatenate(others, axis=0)
    ratio[...] = gammas[low_end // LANES : high_end // LANES, :] * (1.0 / states) / mult_out[...]
    if is_first:
        own = pl.ds(pl.multiple_of(core * rows, rows), rows)
        if away:
            left[:, :away] = jnp.transpose(pair[away:, own])
            left[:, away:] = jnp.transpose(pair[:away, own])
        spread(ratio[own_rows, :], column)
        plain[...] = jnp.zeros_like(plain)
        scaled[...] = jnp.zeros_like(scaled)
    else:
        plain[...] = plain_in[...]
        scaled[...] = scaled_in[...]

    @pl.loop(0, width // tile)
    def _(step):
        columns = pl.ds(pl.multiple_of(step * tile, tile), tile)
        counts = counts_in[:, columns]
        if away:
            counts = counts + jnp.dot(left[...], pair[:, columns], preferred_element_type=jnp.float32)
        counts_out[:, columns] = counts
        ratio_rows = [ratio[pl.ds(step * (tile // LANES) + i, 1), :] for i in range(tile // LANES)]
        add_tile(counts, column[...], ratio_rows, plain, scaled)

    if is_last:
        mult_own = mult_own_ref[own_rows, :]
        terms = gammas[own_rows, :] / mult_own * gathered(plain)
        odds = gathered(scaled) * states / terms
        windows = sent.shape[0] // number

        @pl.loop(0, sent.shape[0])
        def _(target):
            sent[target, :depth] = mult_own
            sent[target, depth:] = jnp.where(lax.rem(target, windows) == window, odds, terms)


def second_kernel(bounds, *refs):
    number_chunks = len(bounds)
    given, gammas = refs[:2]
    mults = refs[2 : 2 + number_chunks]
    counts = refs[2 + number_chunks : 2 + 2 * number_chunks]
    sent, logs_out, state_counts, new_mult, ratio, column, plain, scaled = refs[2 + 2 * number_chunks :]
    depth = logs_out.shape[0]
    states = gammas.shape[0] * LANES
    number = gammas.shape[0] // depth
    windows = given.shape[0] // number
    _, window, core, own_chip = place()
    own_window = lax.broadcasted_iota(jnp.int32, (windows, depth, LANES), 0) == window
    for block in range(number):
        here = pl.ds(pl.multiple_of(lax.rem(block + (number - 2 * own_chip), number) * depth, depth), depth)
        block_mult = given[block * windows : (block + 1) * windows, :depth]
        others = given[block * windows : (block + 1) * windows, depth:]
        part = 2.0 * block_mult / (1.0 + others)
        terms = jnp.where(own_window, part * states, others)
        new_mult[here, :] = jnp.sum(jnp.where(own_window, part * others, 0.0), axis=0)
        total = jnp.sum(block_mult, axis=0)
        state_counts[block * depth : (block + 1) * depth, :] = total
        ratio[here, :] = total / jnp.sum(terms, axis=0)
    raw = ratio[...]
    weights = raw / jnp.sum(raw)
    ratio[...] = gammas[...] * weights / new_mult[...]
    own = pl.ds(pl.multiple_of(core * depth, depth), depth)
    spread(ratio[own, :], column)
    plain[...] = jnp.zeros_like(plain)
    scaled[...] = jnp.zeros_like(scaled)
    for (low_end, high_end), count in zip(bounds, counts):
        width = high_end - low_end
        tile = column_tile(width)

        @pl.loop(0, width // tile)
        def _(step):
            columns = pl.ds(pl.multiple_of(step * tile, tile), tile)
            start = low_end // LANES + step * (tile // LANES)
            ratio_rows = [ratio[pl.ds(start + i, 1), :] for i in range(tile // LANES)]
            add_tile(count[:, columns], column[...], ratio_rows, plain, scaled)

    terms = gammas[own, :] / new_mult[own, :] * gathered(plain)
    window_total = sum(jnp.sum(mult[...]) for mult in mults)
    logs_out[...] = jnp.log(gathered(scaled) * states / window_total)

    @pl.loop(0, sent.shape[0])
    def _(target):
        sent[target] = terms


def last_kernel(given, state_counts, energy_out, raw_ref):
    depth = energy_out.shape[0]
    states = state_counts.shape[0] * LANES
    number = state_counts.shape[0] // depth
    windows = given.shape[0] // number
    for block in range(number):
        here = slice(block * depth, (block + 1) * depth)
        terms = jnp.sum(given[block * windows : (block + 1) * windows], axis=0)
        raw_ref[here, :] = state_counts[here, :] / terms
    total = jnp.sum(raw_ref[...])
    own = pl.ds(pl.multiple_of(place()[0] * depth, depth), depth)
    energy_out[...] = -jnp.log(raw_ref[own, :] / total * states)


def spot(*shape, dtype=jnp.float32):
    return pltpu.VMEM(shape, dtype)


def keep(x):
    return pltpu.with_memory_space_constraint(x, pltpu.VMEM)


def everyone(block):
    return lax.all_to_all(block, ("frames", "win"), 0, 0, tiled=True)


def call(kernel, ins, outs, scratch=(), scalars=(), limit=16, aliases={}, space=pltpu.VMEM):
    smem = pl.BlockSpec(memory_space=pltpu.SMEM)
    vmem = pl.BlockSpec(memory_space=pltpu.VMEM)
    return pl.pallas_call(
        kernel,
        out_shape=tuple(outs),
        in_specs=[smem] * len(scalars) + [pl.BlockSpec(memory_space=space)] * len(ins),
        out_specs=(vmem,) * len(outs),
        scratch_shapes=list(scratch),
        input_output_aliases=aliases,
        compiler_params=pltpu.CompilerParams(vmem_limit_bytes=limit << 20),
    )(*scalars, *ins)


def estimate(memberships, lag_times, segment_ids, bias_codes):
    frames_dev, states = memberships.shape[1:]
    frames_all = segment_ids.shape[1]
    number = lax.axis_size("frames")
    windows = lax.axis_size("win")
    rows = states // number
    depth = rows // LANES
    group = 2 * rows
    bounds = chunk_bounds(states, group)
    near = 2 * frames_dev
    away = frames_all - near
    half = jnp.bfloat16
    codes = bias_codes.reshape(states // LANES, LANES)
    partner = [(i, i ^ 1) for i in range(number)]
    widths = [high - low for low, high in bounds]
    sizes = [widths[0] + LANES] + widths[1:]
    shapes = [spot(frames_dev, states + LANES, dtype=half)]
    for _ in range(1, number // 2):
        shapes += [spot(frames_dev, width, dtype=half) for width in sizes]
    whole, *parts = call(
        lambda *refs: prepare_kernel(group, *refs),
        [memberships],
        shapes,
        [spot(1, frames_dev, states), pltpu.SemaphoreType.DMA((PIECES,))],
        space=pltpu.HBM,
    )
    route = lambda step: [((i + step) % number, i) for i in range(number)]
    across = []
    for chip in range(1, number // 2):
        across.append([])
        for c in range(len(bounds)):
            across[-1].append(lax.ppermute(parts[(chip - 1) * len(bounds) + c], "frames", route(2 * chip)))
    beside = lax.ppermute(whole, "frames", partner)
    inner, outer, joined, gammas = call(
        lambda *refs: plan_kernel(number, group, *refs),
        [segment_ids, codes],
        [
            spot(near, near, dtype=half),
            spot(max(away, 8), frames_all, dtype=half),
            spot(frames_all, frames_all, dtype=half),
            spot(states // LANES, LANES),
        ],
        [
            spot(1, frames_all, dtype=jnp.int32),
            spot(states // LANES, LANES, dtype=jnp.int32),
            pltpu.SemaphoreType.DMA((2,)),
        ],
        scalars=[lag_times],
        space=pltpu.HBM,
    )
    counts = call(
        lambda *refs: near_kernel(bounds, *refs),
        [whole, beside, keep(inner)],
        [spot(rows, width) for width in widths],
        [spot(2 * near, states, dtype=half), spot(rows, 2 * near, dtype=half)],
    )
    counts = list(counts)
    mults = []
    state = [outer, joined] if away else [joined]
    for c, width in enumerate(widths):
        first, last = c == 0, c == len(bounds) - 1
        blocks = [whole, beside]
        for chunk in across:
            arrived = chunk[c]
            if c:
                arrived, state[0] = lax.optimization_barrier((arrived, state[0]))
            blocks += [arrived, lax.ppermute(arrived, "frames", partner)]
        outs = [spot(rows, width), spot(width // LANES, LANES)]
        sums = [spot(rows, LANES), spot(rows, LANES)]
        scratch = []
        if last:
            outs += [spot(number * windows, 2 * depth, LANES)]
            scratch += sums
        else:
            outs += sums
        if first:
            fixed = [spot(rows, LANES), spot(rows, 2 * max(away, 8), dtype=half), spot(48 + away, frames_all, dtype=half)]
            if last:
                scratch += fixed
            else:
                outs += fixed
        scratch += [spot(2 * max(away, 8), width, dtype=half), spot(width // LANES, LANES)]
        results = call(
            lambda *refs, c=c: counts_kernel(bounds, c, number, *refs),
            [keep(gammas), keep(counts[c])] + blocks + [keep(x) for x in state],
            outs,
            scratch,
            aliases={1: 0},
        )
        counts[c] = results[0]
        mults.append(results[1])
        if not last:
            if first:
                fixed = list(results[4:7]) + [results[1]]
            state = list(results[2:4]) + fixed
    sent = results[2]
    given = everyone(sent)
    sums = [spot(states // LANES, LANES)] * 2 + [spot(rows, LANES)] * 3
    sent, logs, state_counts = call(
        lambda *refs: second_kernel(bounds, *refs),
        [given, keep(gammas)] + [keep(x) for x in mults + counts],
        [spot(number * windows, depth, LANES), spot(depth, LANES), spot(states // LANES, LANES)],
        sums,
    )
    given = everyone(sent)
    (energy,) = call(last_kernel, [given, keep(state_counts)], [spot(depth, LANES)], [spot(states // LANES, LANES)])
    return energy.reshape(rows), logs.reshape(1, rows)


def solution(mesh):
    placed = (P("win", "frames", None), P("win"), P("win", None), P("win", None))
    return jax.shard_map(
        estimate,
        mesh=mesh,
        in_specs=placed,
        out_specs=(P("frames"), P("win", "frames")),
        check_vma=False,
    )
```

```python
import math

import jax
import jax.numpy as jnp
from jax import lax
from jax.experimental import pallas as pl
from jax.experimental.pallas import tpu as pltpu
from jax.sharding import PartitionSpec as P


LANES = 128
SAFE = 1.0 / 512.0
BLOCK = 64
ROWS = 256
SPAN = 2048
PIECES = 4

bias_unit = 1.0 / 128.0


def chunk_bounds(states, group):
    return [(0, group), (group, states)] if states > group else [(0, states)]


def granule(states, group):
    size = group
    for low, high in chunk_bounds(states, group):
        size = math.gcd(size, high - low)
    return size


def wrapped(place, states):
    return jnp.where(place >= states, place - states, place)


def split3(x):
    high = x.astype(jnp.bfloat16)
    rest = x - high.astype(jnp.float32)
    middle = rest.astype(jnp.bfloat16)
    low = (rest - middle.astype(jnp.float32)).astype(jnp.bfloat16)
    return high, middle, low


def gamma_of(codes):
    return jnp.exp(codes.astype(jnp.float32) * -bias_unit)


def spread(folded, column_ref):
    for i in range(folded.shape[0]):
        square = jnp.broadcast_to(folded[i : i + 1, :], (LANES, LANES))
        column_ref[i * LANES : (i + 1) * LANES, :] = jnp.transpose(square)


def gathered(partial_ref):
    rows = partial_ref.shape[0]
    return jnp.concatenate(
        [
            jnp.sum(jnp.transpose(partial_ref[i : i + LANES, :]), axis=0, keepdims=True)
            for i in range(0, rows, LANES)
        ],
        axis=0,
    )


def column_tile(width):
    for tile in (512, 256, 128):
        if width % tile == 0:
            return tile


def add_tile(counts_of, column, stiff_rows, plain_ref):
    rows = plain_ref.shape[0]
    for first in range(0, rows, BLOCK):
        here = slice(first, first + BLOCK)
        counts = counts_of(here)
        stiff_col = column[here, :]
        plain = plain_ref[here, :]
        for i, stiff_row in enumerate(stiff_rows):
            plain = plain + counts[:, i * LANES : (i + 1) * LANES] / (stiff_col + stiff_row)
        plain_ref[here, :] = plain


def add_weighted(count, stiff, first, column, partial):
    @pl.loop(0, count.shape[1] // LANES)
    def _(step):
        columns = pl.ds(pl.multiple_of(step * LANES, LANES), LANES)
        stiff_row = stiff[pl.ds(first + step, 1), :]
        partial[...] += count[:, columns] / (column[...] + stiff_row) * stiff_row


def place():
    position = lax.axis_index("frames")
    return position, lax.axis_index("win"), position % 2, position // 2


def fetched(sources, targets, sem):
    copies = [pltpu.make_async_copy(a, b, sem.at[i]) for i, (a, b) in enumerate(zip(sources, targets))]
    for copy in copies:
        copy.start()
    for copy in copies:
        copy.wait()


def prepare_kernel(group, given, *outs):
    member, sem = outs[-2:]
    whole, parts = outs[0], outs[1:-2]
    height = given.shape[1] // PIECES
    pieces = [pl.ds(i * height, height) for i in range(PIECES)]
    fetched([given.at[:, piece, :] for piece in pieces], [member.at[:, piece, :] for piece in pieces], sem)
    frames_dev, states = member.shape[1:]
    bounds = chunk_bounds(states, group)
    size = granule(states, group)
    own_chip = place()[3]
    total = jnp.zeros((frames_dev, LANES), jnp.float32)
    for j in range(0, states, size):
        source = pl.multiple_of(wrapped(own_chip * group + j, states), size)
        block = member[0, :, pl.ds(source, size)].astype(jnp.bfloat16)
        whole[:, j : j + size] = block
        wide = block.astype(jnp.float32)
        for i in range(0, size, LANES):
            total = total + wide[:, i : i + LANES]
    sums = jnp.broadcast_to(jnp.sum(total, axis=1, keepdims=True), (frames_dev, LANES))
    high, middle, low = split3(sums)
    lane = lax.broadcasted_iota(jnp.int32, sums.shape, 1)
    none = jnp.zeros_like(sums)
    packed = jnp.where(lane == 0, high.astype(jnp.float32), none)
    packed = jnp.where(lane == 1, middle.astype(jnp.float32), packed)
    packed = jnp.where(lane == 2, low.astype(jnp.float32), packed).astype(jnp.bfloat16)
    whole[:, states:] = packed
    for chip in range(1, states // group):
        base = (own_chip - chip) * group
        base = jnp.where(base < 0, base + states, base)
        for c, (low_end, high_end) in enumerate(bounds):
            part = parts[(chip - 1) * len(bounds) + c]
            for j in range(low_end, high_end, size):
                source = pl.multiple_of(wrapped(base + j, states), size)
                part[:, j - low_end : j - low_end + size] = member[0, :, pl.ds(source, size)].astype(jnp.bfloat16)
            if c == 0:
                part[:, high_end:] = packed


def plan_kernel(number, group, lag, segments_in, codes_in, inner, outer, joined, gammas, segments, codes, sem):
    fetched([segments_in, codes_in], [segments, codes], sem)
    frames_all = segments.shape[1]
    frames_dev = frames_all // number
    near = 2 * frames_dev
    _, _, core, own_chip = place()
    lag_time = lag[0]
    grid = (frames_all, frames_all)
    row = lax.broadcasted_iota(jnp.int32, grid, 0)
    frame = row
    for i in range(number):
        owner = lax.rem(own_chip + i // 2, number // 2) * 2 + (core if i % 2 == 0 else 1 - core)
        inside = (row >= i * frames_dev) & (row < (i + 1) * frames_dev)
        frame = jnp.where(inside, row + (owner - i) * frames_dev, frame)
    frame = frame.astype(jnp.float32)
    seg_row = jnp.broadcast_to(segments[...].astype(jnp.float32), grid)
    col = lax.broadcasted_iota(jnp.int32, grid, 1).astype(jnp.float32)
    seg = jnp.sum(jnp.where(frame == col, seg_row, 0.0), axis=1, keepdims=True)
    seg_from = jnp.broadcast_to(seg, grid)
    seg_to = jnp.transpose(seg_from)
    frame_to = jnp.transpose(frame)
    ahead = frame_to - frame
    same = seg_from == seg_to
    lag_float = lag_time.astype(jnp.float32)
    forward = same & (ahead == lag_float)
    backward = same & (ahead == -lag_float)
    joined[...] = jnp.where(forward | backward, 1.0, 0.0).astype(jnp.bfloat16)
    forward = jnp.where(forward, 1.0, 0.0)
    inner[...] = forward[:near, :near].astype(jnp.bfloat16)
    if number > 2:
        below = frame < (own_chip * near).astype(jnp.float32)
        touching = jnp.where(below, forward, jnp.where(backward, 1.0, 0.0))
        outer[...] = touching[near:, :].astype(jnp.bfloat16)
    size = granule(codes.shape[0] * LANES, group) // LANES
    for i in range(0, codes.shape[0], size):
        start = wrapped(own_chip * (group // LANES) + i, codes.shape[0])
        gammas[i : i + size, :] = gamma_of(codes[pl.ds(pl.multiple_of(start, size), size), :])


def near_kernel(bounds, whole, beside, inner, *refs):
    counts = refs[: len(bounds)]
    pair, left = refs[len(bounds) :]
    frames_dev = whole.shape[0]
    near = 2 * frames_dev
    rows = left.shape[0]
    states = pair.shape[1]
    own = pl.ds(pl.multiple_of(place()[2] * rows, rows), rows)
    pair[near : near + frames_dev, :] = whole[:, :states]
    pair[near + frames_dev :, :] = beside[:, :states]
    pair[:near, :] = jnp.dot(inner[...], pair[near:, :], preferred_element_type=jnp.float32).astype(jnp.bfloat16)
    left[:, :near] = jnp.transpose(pair[near:, own])
    left[:, near:] = jnp.transpose(pair[:near, own])
    for (low_end, high_end), count in zip(bounds, counts):
        tile = column_tile(high_end - low_end)

        @pl.loop(0, (high_end - low_end) // tile)
        def _(step):
            here = pl.ds(pl.multiple_of(step * tile, tile), tile)
            there = pl.ds(pl.multiple_of(low_end + step * tile, tile), tile)
            count[:, here] = jnp.dot(left[...], pair[:, there], preferred_element_type=jnp.float32)


def counts_kernel(bounds, which, number, *refs):
    low_end, high_end = bounds[which]
    width = high_end - low_end
    is_first, is_last = which == 0, which == len(bounds) - 1
    refs = list(refs)
    take = lambda k: [refs.pop(0) for _ in range(k)]
    gammas, counts_in = take(2)
    blocks = take(number)
    far = number > 2
    if is_first:
        outer, joined = take(2) if far else take(1) * 2
    else:
        plain_in, column, left, outer, earlier_stiff, earlier_mult, earlier_counts = take(7)
    counts_out, mult_out = take(2)
    if is_last:
        (sent,) = take(1)
    else:
        plain, stiff = take(2)
    if is_first:
        column, left, steps = take(3)
    if is_last:
        plain, stiff, rest = take(3)
    (pair,) = take(1)
    frames_dev = blocks[0].shape[0]
    frames_all = number * frames_dev
    away = frames_all - 2 * frames_dev
    rows = plain.shape[0]
    states = gammas.shape[0] * LANES
    depth = rows // LANES
    _, window, core, _ = place()
    own_rows = pl.ds(pl.multiple_of(core * depth, depth), depth)
    tile = column_tile(width)
    if is_first:
        sums = [block[:, states:] for block in blocks[:2]] + [block[:, width:] for block in blocks[2:]]
        column_sums = jnp.dot(joined[...], jnp.concatenate(sums, axis=0), preferred_element_type=jnp.float32)
        turned = jnp.transpose(column_sums)
        line = turned[0:1] + turned[1:2] + turned[2:3]
        parts = [jnp.broadcast_to(part.astype(jnp.float32), (16, frames_all)).astype(jnp.bfloat16) for part in split3(line)]
        steps[:48, :] = jnp.concatenate(parts, axis=0)
        if away:
            steps[48:, :] = outer[...]
        step_matrix = steps
    else:
        step_matrix = outer
    for j in range(0, width, tile):
        local = [block[:, low_end + j : low_end + j + tile] for block in blocks[:2]]
        others = [block[:, j : j + tile] for block in blocks[2:]]
        member = jnp.concatenate(local + others, axis=0)
        product = jnp.dot(step_matrix[...], member, preferred_element_type=jnp.float32)
        mult_row = (product[0:1] + product[16:17] + product[32:33]) * 0.5
        for i in range(tile // LANES):
            mult_out[j // LANES + i : j // LANES + i + 1, :] = mult_row[:, i * LANES : (i + 1) * LANES]
        if away:
            pair[:away, j : j + tile] = product[48:].astype(jnp.bfloat16)
            pair[away:, j : j + tile] = jnp.concatenate(others, axis=0)
    stiff[...] = mult_out[...] / (gammas[low_end // LANES : high_end // LANES, :] * (1.0 / states))
    if is_first:
        own = pl.ds(pl.multiple_of(core * rows, rows), rows)
        if away:
            left[:, :away] = jnp.transpose(pair[away:, own])
            left[:, away:] = jnp.transpose(pair[:away, own])
        spread(stiff[own_rows, :], column)
        plain[...] = jnp.zeros_like(plain)
    else:
        plain[...] = plain_in[...]

    for low in range(0, width, tile):
        columns = slice(low, low + tile)
        product = jnp.dot(left[...], pair[:, columns], preferred_element_type=jnp.float32) if away else None

        def counts_of(here):
            counts = counts_in[here, columns]
            if away:
                counts = counts + product[here]
            counts_out[here, columns] = counts
            return counts

        stiff_rows = [stiff[i : i + 1, :] for i in range(low // LANES, (low + tile) // LANES)]
        add_tile(counts_of, column, stiff_rows, plain)

    if is_last:
        own_mult_ref, own_stiff_ref = (mult_out, stiff) if is_first else (earlier_mult, earlier_stiff)
        mult_own = own_mult_ref[own_rows, :]
        new = own_stiff_ref[own_rows, :] * gathered(plain)
        stiff_refs = [stiff] if is_first else [earlier_stiff, stiff]
        counts_refs = [counts_out] if is_first else [earlier_counts, counts_out]
        whole = mult_own * 2.0
        rest[...] = whole - new

        @pl.when(jnp.min(rest[...] / whole) < SAFE)
        def _():
            plain[...] = jnp.zeros_like(plain)
            for count, stiff_ref in zip(counts_refs, stiff_refs):
                add_weighted(count, stiff_ref, 0, column, plain)
            rest[...] = gathered(plain)

        odds = new / rest[...]
        terms = rest[...] * states
        windows = sent.shape[0] // number

        @pl.loop(0, sent.shape[0])
        def _(target):
            sent[target, :depth] = mult_own
            sent[target, depth:] = jnp.where(lax.rem(target, windows) == window, odds, terms)


def second_kernel(bounds, *refs):
    number_chunks = len(bounds)
    given, gammas = refs[:2]
    mults = refs[2 : 2 + number_chunks]
    counts = refs[2 + number_chunks : 2 + 2 * number_chunks]
    sent, logs_out, state_counts, new_mult, stiff, column, plain, rest = refs[2 + 2 * number_chunks :]
    depth = logs_out.shape[0]
    states = gammas.shape[0] * LANES
    number = gammas.shape[0] // depth
    windows = given.shape[0] // number
    _, window, core, own_chip = place()
    own_window = lax.broadcasted_iota(jnp.int32, (windows, depth, LANES), 0) == window
    for block in range(number):
        here = pl.ds(pl.multiple_of(lax.rem(block + (number - 2 * own_chip), number) * depth, depth), depth)
        block_mult = given[block * windows : (block + 1) * windows, :depth]
        others = given[block * windows : (block + 1) * windows, depth:]
        part = 2.0 * block_mult / (1.0 + others)
        terms = jnp.where(own_window, part * states, others)
        new_mult[here, :] = jnp.sum(jnp.where(own_window, part * others, 0.0), axis=0)
        total = jnp.sum(block_mult, axis=0)
        state_counts[block * depth : (block + 1) * depth, :] = total
        stiff[here, :] = total / jnp.sum(terms, axis=0)
    raw = stiff[...]
    weights = raw / jnp.sum(raw)
    stiff[...] = new_mult[...] / (gammas[...] * weights)
    own = pl.ds(pl.multiple_of(core * depth, depth), depth)
    weights_own = new_mult[own, :] / (stiff[own, :] * gammas[own, :])
    spread(stiff[own, :], column)
    plain[...] = jnp.zeros_like(plain)
    for (low_end, high_end), count in zip(bounds, counts):
        width = high_end - low_end
        for low in range(0, width, SPAN):
            span = min(SPAN, width - low)
            start = (low_end + low) // LANES
            block = min(ROWS, plain.shape[0])

            @pl.loop(0, plain.shape[0] // block)
            def _(step):
                for inner in range(0, block, BLOCK):
                    here = pl.ds(pl.multiple_of(step * block + inner, BLOCK), BLOCK)
                    stiff_col = column[here, :]
                    total = plain[here, :]
                    for i in range(span // LANES):
                        cell = count[here, low + i * LANES : low + (i + 1) * LANES]
                        total = total + cell / (stiff_col + stiff[start + i : start + i + 1, :])
                    plain[here, :] = total

    whole = mults[0][own, :] * 2.0
    new = stiff[own, :] * gathered(plain)
    rest[...] = whole - new

    @pl.when(jnp.min(rest[...] / whole) < SAFE)
    def _():
        plain[...] = jnp.zeros_like(plain)
        for (low_end, _), count in zip(bounds, counts):
            add_weighted(count, stiff, low_end // LANES, column, plain)
        rest[...] = gathered(plain)

    terms = rest[...] / weights_own
    window_total = sum(jnp.sum(mult[...]) for mult in mults)
    logs_out[...] = jnp.log(new * states / window_total)

    @pl.loop(0, sent.shape[0])
    def _(target):
        sent[target] = terms


def last_kernel(given, state_counts, energy_out, raw_ref):
    depth = energy_out.shape[0]
    states = state_counts.shape[0] * LANES
    number = state_counts.shape[0] // depth
    windows = given.shape[0] // number
    for block in range(number):
        here = slice(block * depth, (block + 1) * depth)
        terms = jnp.sum(given[block * windows : (block + 1) * windows], axis=0)
        raw_ref[here, :] = state_counts[here, :] / terms
    total = jnp.sum(raw_ref[...])
    own = pl.ds(pl.multiple_of(place()[0] * depth, depth), depth)
    energy_out[...] = -jnp.log(raw_ref[own, :] / total * states)


def spot(*shape, dtype=jnp.float32):
    return pltpu.VMEM(shape, dtype)


def keep(x):
    return pltpu.with_memory_space_constraint(x, pltpu.VMEM)


def everyone(block):
    return lax.all_to_all(block, ("frames", "win"), 0, 0, tiled=True)


def call(kernel, ins, outs, scratch=(), scalars=(), limit=16, aliases={}, space=pltpu.VMEM):
    smem = pl.BlockSpec(memory_space=pltpu.SMEM)
    vmem = pl.BlockSpec(memory_space=pltpu.VMEM)
    return pl.pallas_call(
        kernel,
        out_shape=tuple(outs),
        in_specs=[smem] * len(scalars) + [pl.BlockSpec(memory_space=space)] * len(ins),
        out_specs=(vmem,) * len(outs),
        scratch_shapes=list(scratch),
        input_output_aliases=aliases,
        compiler_params=pltpu.CompilerParams(vmem_limit_bytes=limit << 20),
    )(*scalars, *ins)


def estimate(memberships, lag_times, segment_ids, bias_codes):
    frames_dev, states = memberships.shape[1:]
    frames_all = segment_ids.shape[1]
    number = lax.axis_size("frames")
    windows = lax.axis_size("win")
    rows = states // number
    depth = rows // LANES
    group = 2 * rows
    bounds = chunk_bounds(states, group)
    near = 2 * frames_dev
    away = frames_all - near
    half = jnp.bfloat16
    codes = bias_codes.reshape(states // LANES, LANES)
    partner = [(i, i ^ 1) for i in range(number)]
    widths = [high - low for low, high in bounds]
    sizes = [widths[0] + LANES] + widths[1:]
    shapes = [spot(frames_dev, states + LANES, dtype=half)]
    for _ in range(1, number // 2):
        shapes += [spot(frames_dev, width, dtype=half) for width in sizes]
    whole, *parts = call(
        lambda *refs: prepare_kernel(group, *refs),
        [memberships],
        shapes,
        [spot(1, frames_dev, states), pltpu.SemaphoreType.DMA((PIECES,))],
        space=pltpu.HBM,
    )
    route = lambda step: [((i + step) % number, i) for i in range(number)]
    across = []
    for chip in range(1, number // 2):
        across.append([])
        for c in range(len(bounds)):
            across[-1].append(lax.ppermute(parts[(chip - 1) * len(bounds) + c], "frames", route(2 * chip)))
    beside = lax.ppermute(whole, "frames", partner)
    inner, outer, joined, gammas = call(
        lambda *refs: plan_kernel(number, group, *refs),
        [segment_ids, codes],
        [
            spot(near, near, dtype=half),
            spot(max(away, 8), frames_all, dtype=half),
            spot(frames_all, frames_all, dtype=half),
            spot(states // LANES, LANES),
        ],
        [
            spot(1, frames_all, dtype=jnp.int32),
            spot(states // LANES, LANES, dtype=jnp.int32),
            pltpu.SemaphoreType.DMA((2,)),
        ],
        scalars=[lag_times],
        space=pltpu.HBM,
    )
    counts = call(
        lambda *refs: near_kernel(bounds, *refs),
        [whole, beside, keep(inner)],
        [spot(rows, width) for width in widths],
        [spot(2 * near, states, dtype=half), spot(rows, 2 * near, dtype=half)],
    )
    counts = list(counts)
    mults = []
    state = [outer, joined] if away else [joined]
    for c, width in enumerate(widths):
        first, last = c == 0, c == len(bounds) - 1
        blocks = [whole, beside]
        for chunk in across:
            arrived = chunk[c]
            if c:
                arrived, state[0] = lax.optimization_barrier((arrived, state[0]))
            blocks += [arrived, lax.ppermute(arrived, "frames", partner)]
        outs = [spot(rows, width), spot(width // LANES, LANES)]
        sums = [spot(rows, LANES), spot(width // LANES, LANES)]
        scratch = []
        if last:
            outs += [spot(number * windows, 2 * depth, LANES)]
        else:
            outs += sums
        fixed = [spot(rows, LANES), spot(rows, 2 * max(away, 8), dtype=half), spot(48 + away, frames_all, dtype=half)]
        if first:
            if last:
                scratch += fixed
            else:
                outs += fixed
        if last:
            scratch += sums + [spot(depth, LANES)]
        scratch += [spot(2 * max(away, 8), width, dtype=half)]
        results = call(
            lambda *refs, c=c: counts_kernel(bounds, c, number, *refs),
            [keep(gammas), keep(counts[c])] + blocks + [keep(x) for x in state],
            outs,
            scratch,
        )
        counts[c] = results[0]
        mults.append(results[1])
        if not last:
            state = [results[2]] + list(results[4:7]) + [results[3], results[1], results[0]]
    sent = results[2]
    given = everyone(sent)
    sums = [spot(states // LANES, LANES)] * 2 + [spot(rows, LANES)] * 2 + [spot(depth, LANES)]
    sent, logs, state_counts = call(
        lambda *refs: second_kernel(bounds, *refs),
        [given, keep(gammas)] + [keep(x) for x in mults + counts],
        [spot(number * windows, depth, LANES), spot(depth, LANES), spot(states // LANES, LANES)],
        sums,
    )
    given = everyone(sent)
    (energy,) = call(last_kernel, [given, keep(state_counts)], [spot(depth, LANES)], [spot(states // LANES, LANES)])
    return energy.reshape(rows), logs.reshape(1, rows)


def solution(mesh):
    placed = (P("win", "frames", None), P("win"), P("win", None), P("win", None))
    return jax.shard_map(
        estimate,
        mesh=mesh,
        in_specs=placed,
        out_specs=(P("frames"), P("win", "frames")),
        check_vma=False,
    )
```

```python
import math

import jax
import jax.numpy as jnp
from jax import lax
from jax.experimental import pallas as pl
from jax.experimental.pallas import tpu as pltpu
from jax.sharding import PartitionSpec as P


LANES = 128
SAFE = 1.0 / 512.0
BLOCK = 64
ROWS = 256
SPAN = 2048
PIECES = 4

bias_unit = 1.0 / 128.0


def chunk_bounds(states, group):
    return [(0, group), (group, states)] if states > group else [(0, states)]


def granule(states, group):
    size = group
    for low, high in chunk_bounds(states, group):
        size = math.gcd(size, high - low)
    return size


def wrapped(place, states):
    return jnp.where(place >= states, place - states, place)


def split3(x):
    high = x.astype(jnp.bfloat16)
    rest = x - high.astype(jnp.float32)
    middle = rest.astype(jnp.bfloat16)
    low = (rest - middle.astype(jnp.float32)).astype(jnp.bfloat16)
    return high, middle, low


def gamma_of(codes):
    return jnp.exp(codes.astype(jnp.float32) * -bias_unit)


def spread(folded, column_ref):
    for i in range(folded.shape[0]):
        square = jnp.broadcast_to(folded[i : i + 1, :], (LANES, LANES))
        column_ref[i * LANES : (i + 1) * LANES, :] = jnp.transpose(square)


def gathered(partial_ref):
    rows = partial_ref.shape[0]
    return jnp.concatenate(
        [
            jnp.sum(jnp.transpose(partial_ref[i : i + LANES, :]), axis=0, keepdims=True)
            for i in range(0, rows, LANES)
        ],
        axis=0,
    )


def column_tile(width):
    for tile in (512, 256, 128):
        if width % tile == 0:
            return tile


def add_tile(counts_of, column, stiff_rows, plain_ref):
    rows = plain_ref.shape[0]
    for first in range(0, rows, BLOCK):
        here = slice(first, first + BLOCK)
        counts = counts_of(here)
        stiff_col = column[here, :]
        plain = plain_ref[here, :]
        for i, stiff_row in enumerate(stiff_rows):
            plain = plain + counts[:, i * LANES : (i + 1) * LANES] / (stiff_col + stiff_row)
        plain_ref[here, :] = plain


def add_weighted(count, stiff, first, column, partial):
    @pl.loop(0, count.shape[1] // LANES)
    def _(step):
        columns = pl.ds(pl.multiple_of(step * LANES, LANES), LANES)
        stiff_row = stiff[pl.ds(first + step, 1), :]
        partial[...] += count[:, columns] / (column[...] + stiff_row) * stiff_row


def each(number, put):
    if number <= 64:
        for target in range(number):
            put(target)
    else:
        pl.loop(0, number)(put)


def place():
    position = lax.axis_index("frames")
    return position, lax.axis_index("win"), position % 2, position // 2


def fetched(sources, targets, sem):
    copies = [pltpu.make_async_copy(a, b, sem.at[i]) for i, (a, b) in enumerate(zip(sources, targets))]
    for copy in copies:
        copy.start()
    for copy in copies:
        copy.wait()


def prepare_kernel(group, given, *outs):
    member, sem = outs[-2:]
    whole, parts = outs[0], outs[1:-2]
    height = given.shape[1] // PIECES
    pieces = [pl.ds(i * height, height) for i in range(PIECES)]
    fetched([given.at[:, piece, :] for piece in pieces], [member.at[:, piece, :] for piece in pieces], sem)
    frames_dev, states = member.shape[1:]
    bounds = chunk_bounds(states, group)
    size = granule(states, group)
    own_chip = place()[3]
    total = jnp.zeros((frames_dev, LANES), jnp.float32)
    for j in range(0, states, size):
        source = pl.multiple_of(wrapped(own_chip * group + j, states), size)
        block = member[0, :, pl.ds(source, size)].astype(jnp.bfloat16)
        whole[:, j : j + size] = block
        wide = block.astype(jnp.float32)
        for i in range(0, size, LANES):
            total = total + wide[:, i : i + LANES]
    sums = jnp.broadcast_to(jnp.sum(total, axis=1, keepdims=True), (frames_dev, LANES))
    high, middle, low = split3(sums)
    lane = lax.broadcasted_iota(jnp.int32, sums.shape, 1)
    none = jnp.zeros_like(sums)
    packed = jnp.where(lane == 0, high.astype(jnp.float32), none)
    packed = jnp.where(lane == 1, middle.astype(jnp.float32), packed)
    packed = jnp.where(lane == 2, low.astype(jnp.float32), packed).astype(jnp.bfloat16)
    whole[:, states:] = packed
    for chip in range(1, states // group):
        base = (own_chip - chip) * group
        base = jnp.where(base < 0, base + states, base)
        for c, (low_end, high_end) in enumerate(bounds):
            part = parts[(chip - 1) * len(bounds) + c]
            for j in range(low_end, high_end, size):
                source = pl.multiple_of(wrapped(base + j, states), size)
                part[:, j - low_end : j - low_end + size] = member[0, :, pl.ds(source, size)].astype(jnp.bfloat16)
            if c == 0:
                part[:, high_end:] = packed


def plan_kernel(number, group, lag, segments_in, codes_in, inner, outer, joined, gammas, segments, codes, sem):
    fetched([segments_in, codes_in], [segments, codes], sem)
    frames_all = segments.shape[1]
    frames_dev = frames_all // number
    near = 2 * frames_dev
    _, _, core, own_chip = place()
    lag_time = lag[0]
    grid = (frames_all, frames_all)
    row = lax.broadcasted_iota(jnp.int32, grid, 0)
    frame = row
    for i in range(number):
        owner = lax.rem(own_chip + i // 2, number // 2) * 2 + (core if i % 2 == 0 else 1 - core)
        inside = (row >= i * frames_dev) & (row < (i + 1) * frames_dev)
        frame = jnp.where(inside, row + (owner - i) * frames_dev, frame)
    frame = frame.astype(jnp.float32)
    seg_row = jnp.broadcast_to(segments[...].astype(jnp.float32), grid)
    col = lax.broadcasted_iota(jnp.int32, grid, 1).astype(jnp.float32)
    seg = jnp.sum(jnp.where(frame == col, seg_row, 0.0), axis=1, keepdims=True)
    seg_from = jnp.broadcast_to(seg, grid)
    seg_to = jnp.transpose(seg_from)
    frame_to = jnp.transpose(frame)
    ahead = frame_to - frame
    same = seg_from == seg_to
    lag_float = lag_time.astype(jnp.float32)
    forward = same & (ahead == lag_float)
    backward = same & (ahead == -lag_float)
    joined[...] = jnp.where(forward | backward, 1.0, 0.0).astype(jnp.bfloat16)
    forward = jnp.where(forward, 1.0, 0.0)
    inner[...] = forward[:near, :near].astype(jnp.bfloat16)
    if number > 2:
        below = frame < (own_chip * near).astype(jnp.float32)
        touching = jnp.where(below, forward, jnp.where(backward, 1.0, 0.0))
        outer[...] = touching[near:, :].astype(jnp.bfloat16)
    size = granule(codes.shape[0] * LANES, group) // LANES
    for i in range(0, codes.shape[0], size):
        start = wrapped(own_chip * (group // LANES) + i, codes.shape[0])
        gammas[i : i + size, :] = gamma_of(codes[pl.ds(pl.multiple_of(start, size), size), :])


def near_kernel(bounds, whole, beside, inner, *refs):
    counts = refs[: len(bounds)]
    pair, left = refs[len(bounds) :]
    frames_dev = whole.shape[0]
    near = 2 * frames_dev
    rows = left.shape[0]
    states = pair.shape[1]
    own = pl.ds(pl.multiple_of(place()[2] * rows, rows), rows)
    pair[near : near + frames_dev, :] = whole[:, :states]
    pair[near + frames_dev :, :] = beside[:, :states]
    pair[:near, :] = jnp.dot(inner[...], pair[near:, :], preferred_element_type=jnp.float32).astype(jnp.bfloat16)
    left[:, :near] = jnp.transpose(pair[near:, own])
    left[:, near:] = jnp.transpose(pair[:near, own])
    for (low_end, high_end), count in zip(bounds, counts):
        tile = column_tile(high_end - low_end)

        @pl.loop(0, (high_end - low_end) // tile)
        def _(step):
            here = pl.ds(pl.multiple_of(step * tile, tile), tile)
            there = pl.ds(pl.multiple_of(low_end + step * tile, tile), tile)
            count[:, here] = jnp.dot(left[...], pair[:, there], preferred_element_type=jnp.float32)


def counts_kernel(bounds, which, number, *refs):
    low_end, high_end = bounds[which]
    width = high_end - low_end
    is_first, is_last = which == 0, which == len(bounds) - 1
    refs = list(refs)
    take = lambda k: [refs.pop(0) for _ in range(k)]
    gammas, counts_in = take(2)
    blocks = take(number)
    far = number > 2
    if is_first:
        outer, joined = take(2) if far else take(1) * 2
    else:
        plain_in, column, left, outer, earlier_stiff, earlier_mult, earlier_counts = take(7)
    counts_out, mult_out = take(2)
    if is_last:
        (sent,) = take(1)
    else:
        plain, stiff = take(2)
    if is_first:
        column, left, steps = take(3)
    if is_last:
        plain, stiff, rest = take(3)
    (pair,) = take(1)
    frames_dev = blocks[0].shape[0]
    frames_all = number * frames_dev
    away = frames_all - 2 * frames_dev
    rows = plain.shape[0]
    states = gammas.shape[0] * LANES
    depth = rows // LANES
    _, window, core, _ = place()
    own_rows = pl.ds(pl.multiple_of(core * depth, depth), depth)
    tile = column_tile(width)
    if is_first:
        sums = [block[:, states:] for block in blocks[:2]] + [block[:, width:] for block in blocks[2:]]
        column_sums = jnp.dot(joined[...], jnp.concatenate(sums, axis=0), preferred_element_type=jnp.float32)
        turned = jnp.transpose(column_sums)
        line = turned[0:1] + turned[1:2] + turned[2:3]
        parts = [jnp.broadcast_to(part.astype(jnp.float32), (16, frames_all)).astype(jnp.bfloat16) for part in split3(line)]
        steps[:48, :] = jnp.concatenate(parts, axis=0)
        if away:
            steps[48:, :] = outer[...]
        step_matrix = steps
    else:
        step_matrix = outer
    for j in range(0, width, tile):
        local = [block[:, low_end + j : low_end + j + tile] for block in blocks[:2]]
        others = [block[:, j : j + tile] for block in blocks[2:]]
        member = jnp.concatenate(local + others, axis=0)
        product = jnp.dot(step_matrix[...], member, preferred_element_type=jnp.float32)
        mult_row = (product[0:1] + product[16:17] + product[32:33]) * 0.5
        for i in range(tile // LANES):
            mult_out[j // LANES + i : j // LANES + i + 1, :] = mult_row[:, i * LANES : (i + 1) * LANES]
        if away:
            pair[:away, j : j + tile] = product[48:].astype(jnp.bfloat16)
            pair[away:, j : j + tile] = jnp.concatenate(others, axis=0)
    stiff[...] = mult_out[...] / (gammas[low_end // LANES : high_end // LANES, :] * (1.0 / states))
    if is_first:
        own = pl.ds(pl.multiple_of(core * rows, rows), rows)
        if away:
            left[:, :away] = jnp.transpose(pair[away:, own])
            left[:, away:] = jnp.transpose(pair[:away, own])
        spread(stiff[own_rows, :], column)
        plain[...] = jnp.zeros_like(plain)
    else:
        plain[...] = plain_in[...]

    if is_last:
        mult_own = (mult_out if is_first else earlier_mult)[own_rows, :]

        def put_mult(target):
            sent[target, :depth] = mult_own

        each(sent.shape[0], put_mult)
    for low in range(0, width, tile):
        columns = slice(low, low + tile)
        product = jnp.dot(left[...], pair[:, columns], preferred_element_type=jnp.float32) if away else None

        def counts_of(here):
            counts = counts_in[here, columns]
            if away:
                counts = counts + product[here]
            counts_out[here, columns] = counts
            return counts

        stiff_rows = [stiff[i : i + 1, :] for i in range(low // LANES, (low + tile) // LANES)]
        add_tile(counts_of, column, stiff_rows, plain)

    if is_last:
        own_stiff_ref = stiff if is_first else earlier_stiff
        new = own_stiff_ref[own_rows, :] * gathered(plain)
        stiff_refs = [stiff] if is_first else [earlier_stiff, stiff]
        counts_refs = [counts_out] if is_first else [earlier_counts, counts_out]
        whole = mult_own * 2.0
        rest[...] = whole - new

        @pl.when(jnp.min(rest[...] / whole) < SAFE)
        def _():
            plain[...] = jnp.zeros_like(plain)
            for count, stiff_ref in zip(counts_refs, stiff_refs):
                add_weighted(count, stiff_ref, 0, column, plain)
            rest[...] = gathered(plain)

        odds = new / rest[...]
        terms = rest[...] * states
        windows = sent.shape[0] // number

        def put_rest(target):
            sent[target, depth:] = jnp.where(lax.rem(target, windows) == window, odds, terms)

        each(sent.shape[0], put_rest)


def second_kernel(bounds, *refs):
    number_chunks = len(bounds)
    given, gammas = refs[:2]
    mults = refs[2 : 2 + number_chunks]
    counts = refs[2 + number_chunks : 2 + 2 * number_chunks]
    sent, logs_out, state_counts, new_mult, stiff, column, plain, rest = refs[2 + 2 * number_chunks :]
    depth = logs_out.shape[1] // LANES
    states = gammas.shape[0] * LANES
    number = gammas.shape[0] // depth
    windows = given.shape[0] // number
    _, window, core, own_chip = place()
    own_window = lax.broadcasted_iota(jnp.int32, (windows, depth, LANES), 0) == window
    for block in range(number):
        here = pl.ds(pl.multiple_of(lax.rem(block + (number - 2 * own_chip), number) * depth, depth), depth)
        block_mult = given[block * windows : (block + 1) * windows, :depth]
        others = given[block * windows : (block + 1) * windows, depth:]
        part = 2.0 * block_mult / (1.0 + others)
        terms = jnp.where(own_window, part * states, others)
        new_mult[here, :] = jnp.sum(jnp.where(own_window, part * others, 0.0), axis=0)
        total = jnp.sum(block_mult, axis=0)
        state_counts[block * depth : (block + 1) * depth, :] = total
        stiff[here, :] = total / jnp.sum(terms, axis=0)
    raw = stiff[...]
    weights = raw / jnp.sum(raw)
    stiff[...] = new_mult[...] / (gammas[...] * weights)
    own = pl.ds(pl.multiple_of(core * depth, depth), depth)
    weights_own = new_mult[own, :] / (stiff[own, :] * gammas[own, :])
    spread(stiff[own, :], column)
    plain[...] = jnp.zeros_like(plain)
    for (low_end, high_end), count in zip(bounds, counts):
        width = high_end - low_end
        for low in range(0, width, SPAN):
            span = min(SPAN, width - low)
            start = (low_end + low) // LANES
            block = min(ROWS, plain.shape[0])

            @pl.loop(0, plain.shape[0] // block)
            def _(step):
                for inner in range(0, block, BLOCK):
                    here = pl.ds(pl.multiple_of(step * block + inner, BLOCK), BLOCK)
                    stiff_col = column[here, :]
                    total = plain[here, :]
                    for i in range(span // LANES):
                        cell = count[here, low + i * LANES : low + (i + 1) * LANES]
                        total = total + cell / (stiff_col + stiff[start + i : start + i + 1, :])
                    plain[here, :] = total

    whole = mults[0][own, :] * 2.0
    new = stiff[own, :] * gathered(plain)
    rest[...] = whole - new

    @pl.when(jnp.min(rest[...] / whole) < SAFE)
    def _():
        plain[...] = jnp.zeros_like(plain)
        for (low_end, _), count in zip(bounds, counts):
            add_weighted(count, stiff, low_end // LANES, column, plain)
        rest[...] = gathered(plain)

    terms = rest[...] / weights_own
    window_total = sum(jnp.sum(mult[...]) for mult in mults)
    logs = jnp.log(new * states / window_total)
    for i in range(depth):
        logs_out[:, i * LANES : (i + 1) * LANES] = logs[i : i + 1, :]

    def put(target):
        sent[target] = terms

    each(sent.shape[0], put)


def last_kernel(given, state_counts, energy_out, raw_ref):
    depth = energy_out.shape[0] // LANES
    states = state_counts.shape[0] * LANES
    number = state_counts.shape[0] // depth
    windows = given.shape[0] // number
    for block in range(number):
        here = slice(block * depth, (block + 1) * depth)
        terms = jnp.sum(given[block * windows : (block + 1) * windows], axis=0)
        raw_ref[here, :] = state_counts[here, :] / terms
    total = jnp.sum(raw_ref[...])
    own = pl.ds(pl.multiple_of(place()[0] * depth, depth), depth)
    energy = -jnp.log(raw_ref[own, :] / total * states)
    for i in range(depth):
        energy_out[i * LANES : (i + 1) * LANES] = energy[i]


def spot(*shape, dtype=jnp.float32):
    return pltpu.VMEM(shape, dtype)


def keep(x):
    return pltpu.with_memory_space_constraint(x, pltpu.VMEM)


def everyone(block):
    return lax.all_to_all(block, ("frames", "win"), 0, 0, tiled=True)


def call(kernel, ins, outs, scratch=(), scalars=(), limit=16, aliases={}, space=pltpu.VMEM):
    smem = pl.BlockSpec(memory_space=pltpu.SMEM)
    vmem = pl.BlockSpec(memory_space=pltpu.VMEM)
    return pl.pallas_call(
        kernel,
        out_shape=tuple(outs),
        in_specs=[smem] * len(scalars) + [pl.BlockSpec(memory_space=space)] * len(ins),
        out_specs=(vmem,) * len(outs),
        scratch_shapes=list(scratch),
        input_output_aliases=aliases,
        compiler_params=pltpu.CompilerParams(vmem_limit_bytes=limit << 20),
    )(*scalars, *ins)


def estimate(memberships, lag_times, segment_ids, bias_codes):
    frames_dev, states = memberships.shape[1:]
    frames_all = segment_ids.shape[1]
    number = lax.axis_size("frames")
    windows = lax.axis_size("win")
    rows = states // number
    depth = rows // LANES
    group = 2 * rows
    bounds = chunk_bounds(states, group)
    near = 2 * frames_dev
    away = frames_all - near
    half = jnp.bfloat16
    codes = bias_codes.reshape(states // LANES, LANES)
    partner = [(i, i ^ 1) for i in range(number)]
    widths = [high - low for low, high in bounds]
    sizes = [widths[0] + LANES] + widths[1:]
    shapes = [spot(frames_dev, states + LANES, dtype=half)]
    for _ in range(1, number // 2):
        shapes += [spot(frames_dev, width, dtype=half) for width in sizes]
    whole, *parts = call(
        lambda *refs: prepare_kernel(group, *refs),
        [pltpu.with_memory_space_constraint(memberships, pltpu.HBM)],
        shapes,
        [spot(1, frames_dev, states), pltpu.SemaphoreType.DMA((PIECES,))],
        space=pltpu.HBM,
    )
    route = lambda step: [((i + step) % number, i) for i in range(number)]
    across = []
    for chip in range(1, number // 2):
        across.append([])
        for c in range(len(bounds)):
            across[-1].append(lax.ppermute(parts[(chip - 1) * len(bounds) + c], "frames", route(2 * chip)))
    beside = lax.ppermute(whole, "frames", partner)
    inner, outer, joined, gammas = call(
        lambda *refs: plan_kernel(number, group, *refs),
        [pltpu.with_memory_space_constraint(x, pltpu.HBM) for x in (segment_ids, codes)],
        [
            spot(near, near, dtype=half),
            spot(max(away, 8), frames_all, dtype=half),
            spot(frames_all, frames_all, dtype=half),
            spot(states // LANES, LANES),
        ],
        [
            spot(1, frames_all, dtype=jnp.int32),
            spot(states // LANES, LANES, dtype=jnp.int32),
            pltpu.SemaphoreType.DMA((2,)),
        ],
        scalars=[lag_times],
        space=pltpu.HBM,
    )
    counts = call(
        lambda *refs: near_kernel(bounds, *refs),
        [whole, beside, keep(inner)],
        [spot(rows, width) for width in widths],
        [spot(2 * near, states, dtype=half), spot(rows, 2 * near, dtype=half)],
    )
    counts = list(counts)
    mults = []
    state = [outer, joined] if away else [joined]
    for c, width in enumerate(widths):
        first, last = c == 0, c == len(bounds) - 1
        blocks = [whole, beside]
        for chunk in across:
            arrived = chunk[c]
            if c:
                arrived, state[0] = lax.optimization_barrier((arrived, state[0]))
            blocks += [arrived, lax.ppermute(arrived, "frames", partner)]
        outs = [spot(rows, width), spot(width // LANES, LANES)]
        sums = [spot(rows, LANES), spot(width // LANES, LANES)]
        scratch = []
        if last:
            outs += [spot(number * windows, 2 * depth, LANES)]
        else:
            outs += sums
        fixed = [spot(rows, LANES), spot(rows, 2 * max(away, 8), dtype=half), spot(48 + away, frames_all, dtype=half)]
        if first:
            if last:
                scratch += fixed
            else:
                outs += fixed
        if last:
            scratch += sums + [spot(depth, LANES)]
        scratch += [spot(2 * max(away, 8), width, dtype=half)]
        results = call(
            lambda *refs, c=c: counts_kernel(bounds, c, number, *refs),
            [keep(gammas), keep(counts[c])] + blocks + [keep(x) for x in state],
            outs,
            scratch,
        )
        counts[c] = results[0]
        mults.append(results[1])
        if not last:
            state = [results[2]] + list(results[4:7]) + [results[3], results[1], results[0]]
    sent = results[2]
    given = everyone(sent)
    sums = [spot(states // LANES, LANES)] * 2 + [spot(rows, LANES)] * 2 + [spot(depth, LANES)]
    sent, logs, state_counts = call(
        lambda *refs: second_kernel(bounds, *refs),
        [given, keep(gammas)] + [keep(x) for x in mults + counts],
        [
            spot(number * windows, depth, LANES),
            jax.ShapeDtypeStruct((1, rows), jnp.float32),
            spot(states // LANES, LANES),
        ],
        sums,
    )
    given = everyone(sent)
    (energy,) = call(
        last_kernel,
        [given, keep(state_counts)],
        [jax.ShapeDtypeStruct((rows,), jnp.float32)],
        [spot(states // LANES, LANES)],
    )
    return energy, logs


def solution(mesh):
    placed = (P("win", "frames", None), P("win"), P("win", None), P("win", None))
    return jax.shard_map(
        estimate,
        mesh=mesh,
        in_specs=placed,
        out_specs=(P("frames"), P("win", "frames")),
        check_vma=False,
    )
```

```python
import math

import jax
import jax.numpy as jnp
from jax import lax
from jax.experimental import pallas as pl
from jax.experimental.pallas import tpu as pltpu
from jax.sharding import PartitionSpec as P


LANES = 128
SAFE = 1.0 / 512.0
BLOCK = 64
ROWS = 256
SPAN = 2048
PIECES = 4

bias_unit = 1.0 / 128.0


def chunk_bounds(states, group):
    return [(0, group), (group, states)] if states > group else [(0, states)]


def granule(states, group):
    size = group
    for low, high in chunk_bounds(states, group):
        size = math.gcd(size, high - low)
    return size


def wrapped(place, states):
    return jnp.where(place >= states, place - states, place)


def split3(x):
    high = x.astype(jnp.bfloat16)
    rest = x - high.astype(jnp.float32)
    middle = rest.astype(jnp.bfloat16)
    low = (rest - middle.astype(jnp.float32)).astype(jnp.bfloat16)
    return high, middle, low


def gamma_of(codes):
    return jnp.exp(codes.astype(jnp.float32) * -bias_unit)


def spread(folded, column_ref):
    for i in range(folded.shape[0]):
        square = jnp.broadcast_to(folded[i : i + 1, :], (LANES, LANES))
        column_ref[i * LANES : (i + 1) * LANES, :] = jnp.transpose(square)


def gathered(partial_ref):
    rows = partial_ref.shape[0]
    return jnp.concatenate(
        [
            jnp.sum(jnp.transpose(partial_ref[i : i + LANES, :]), axis=0, keepdims=True)
            for i in range(0, rows, LANES)
        ],
        axis=0,
    )


def column_tile(width):
    for tile in (512, 256, 128):
        if width % tile == 0:
            return tile


def add_tile(counts_of, column, stiff_rows, plain_ref):
    rows = plain_ref.shape[0]
    for first in range(0, rows, BLOCK):
        here = slice(first, first + BLOCK)
        counts = counts_of(here)
        stiff_col = column[here, :]
        plain = plain_ref[here, :]
        for i, stiff_row in enumerate(stiff_rows):
            plain = plain + counts[:, i * LANES : (i + 1) * LANES] / (stiff_col + stiff_row)
        plain_ref[here, :] = plain


def add_weighted(count, stiff, first, column, partial):
    @pl.loop(0, count.shape[1] // LANES)
    def _(step):
        columns = pl.ds(pl.multiple_of(step * LANES, LANES), LANES)
        stiff_row = stiff[pl.ds(first + step, 1), :]
        partial[...] += count[:, columns] / (column[...] + stiff_row) * stiff_row


def each(number, put):
    if number <= 64:
        for target in range(number):
            put(target)
    else:
        pl.loop(0, number)(put)


def place():
    position = lax.axis_index("frames")
    return position, lax.axis_index("win"), position % 2, position // 2


def fetched(sources, targets, sem):
    copies = [pltpu.make_async_copy(a, b, sem.at[i]) for i, (a, b) in enumerate(zip(sources, targets))]
    for copy in copies:
        copy.start()
    for copy in copies:
        copy.wait()


def prepare_kernel(group, given, *outs):
    member, sem = outs[-2:]
    whole, parts = outs[0], outs[1:-2]
    height = given.shape[1] // PIECES
    pieces = [pl.ds(i * height, height) for i in range(PIECES)]
    fetched([given.at[:, piece, :] for piece in pieces], [member.at[:, piece, :] for piece in pieces], sem)
    frames_dev, states = member.shape[1:]
    bounds = chunk_bounds(states, group)
    size = granule(states, group)
    own_chip = place()[3]
    total = jnp.zeros((frames_dev, LANES), jnp.float32)
    for j in range(0, states, size):
        source = pl.multiple_of(wrapped(own_chip * group + j, states), size)
        block = member[0, :, pl.ds(source, size)].astype(jnp.bfloat16)
        whole[:, j : j + size] = block
        wide = block.astype(jnp.float32)
        for i in range(0, size, LANES):
            total = total + wide[:, i : i + LANES]
    sums = jnp.broadcast_to(jnp.sum(total, axis=1, keepdims=True), (frames_dev, LANES))
    high, middle, low = split3(sums)
    lane = lax.broadcasted_iota(jnp.int32, sums.shape, 1)
    none = jnp.zeros_like(sums)
    packed = jnp.where(lane == 0, high.astype(jnp.float32), none)
    packed = jnp.where(lane == 1, middle.astype(jnp.float32), packed)
    packed = jnp.where(lane == 2, low.astype(jnp.float32), packed).astype(jnp.bfloat16)
    whole[:, states:] = packed
    for chip in range(1, states // group):
        base = (own_chip - chip) * group
        base = jnp.where(base < 0, base + states, base)
        for c, (low_end, high_end) in enumerate(bounds):
            part = parts[(chip - 1) * len(bounds) + c]
            for j in range(low_end, high_end, size):
                source = pl.multiple_of(wrapped(base + j, states), size)
                part[:, j - low_end : j - low_end + size] = member[0, :, pl.ds(source, size)].astype(jnp.bfloat16)
            if c == 0:
                part[:, high_end:] = packed


def plan_kernel(number, group, lag, segments_in, codes_in, inner, outer, joined, gammas, segments, codes, sem):
    fetched([segments_in, codes_in], [segments, codes], sem)
    frames_all = segments.shape[1]
    frames_dev = frames_all // number
    near = 2 * frames_dev
    _, _, core, own_chip = place()
    lag_time = lag[0]
    grid = (frames_all, frames_all)
    row = lax.broadcasted_iota(jnp.int32, grid, 0)
    frame = row
    for i in range(number):
        owner = lax.rem(own_chip + i // 2, number // 2) * 2 + (core if i % 2 == 0 else 1 - core)
        inside = (row >= i * frames_dev) & (row < (i + 1) * frames_dev)
        frame = jnp.where(inside, row + (owner - i) * frames_dev, frame)
    frame = frame.astype(jnp.float32)
    seg_row = jnp.broadcast_to(segments[...].astype(jnp.float32), grid)
    col = lax.broadcasted_iota(jnp.int32, grid, 1).astype(jnp.float32)
    seg = jnp.sum(jnp.where(frame == col, seg_row, 0.0), axis=1, keepdims=True)
    seg_from = jnp.broadcast_to(seg, grid)
    seg_to = jnp.transpose(seg_from)
    frame_to = jnp.transpose(frame)
    ahead = frame_to - frame
    same = seg_from == seg_to
    lag_float = lag_time.astype(jnp.float32)
    forward = same & (ahead == lag_float)
    backward = same & (ahead == -lag_float)
    joined[...] = jnp.where(forward | backward, 1.0, 0.0).astype(jnp.bfloat16)
    forward = jnp.where(forward, 1.0, 0.0)
    inner[...] = forward[:near, :near].astype(jnp.bfloat16)
    if number > 2:
        below = frame < (own_chip * near).astype(jnp.float32)
        touching = jnp.where(below, forward, jnp.where(backward, 1.0, 0.0))
        outer[...] = touching[near:, :].astype(jnp.bfloat16)
    size = granule(codes.shape[0] * LANES, group) // LANES
    for i in range(0, codes.shape[0], size):
        start = wrapped(own_chip * (group // LANES) + i, codes.shape[0])
        gammas[i : i + size, :] = gamma_of(codes[pl.ds(pl.multiple_of(start, size), size), :])


def near_kernel(bounds, whole, beside, inner, *refs):
    counts = refs[: len(bounds)]
    pair, left = refs[len(bounds) :]
    frames_dev = whole.shape[0]
    near = 2 * frames_dev
    rows = left.shape[0]
    states = pair.shape[1]
    own = pl.ds(pl.multiple_of(place()[2] * rows, rows), rows)
    pair[near : near + frames_dev, :] = whole[:, :states]
    pair[near + frames_dev :, :] = beside[:, :states]
    pair[:near, :] = jnp.dot(inner[...], pair[near:, :], preferred_element_type=jnp.float32).astype(jnp.bfloat16)
    left[:, :near] = jnp.transpose(pair[near:, own])
    left[:, near:] = jnp.transpose(pair[:near, own])
    for (low_end, high_end), count in zip(bounds, counts):
        tile = column_tile(high_end - low_end)

        @pl.loop(0, (high_end - low_end) // tile)
        def _(step):
            here = pl.ds(pl.multiple_of(step * tile, tile), tile)
            there = pl.ds(pl.multiple_of(low_end + step * tile, tile), tile)
            count[:, here] = jnp.dot(left[...], pair[:, there], preferred_element_type=jnp.float32)


def counts_kernel(bounds, which, number, *refs):
    low_end, high_end = bounds[which]
    width = high_end - low_end
    is_first, is_last = which == 0, which == len(bounds) - 1
    refs = list(refs)
    take = lambda k: [refs.pop(0) for _ in range(k)]
    gammas, counts_in = take(2)
    blocks = take(number)
    far = number > 2
    if is_first:
        outer, joined = take(2) if far else take(1) * 2
    else:
        plain_in, column, left, outer, earlier_stiff, earlier_mult, earlier_counts = take(7)
    counts_out, mult_out = take(2)
    if is_last:
        (sent,) = take(1)
    else:
        plain, stiff = take(2)
    if is_first:
        column, left, steps = take(3)
    if is_last:
        plain, stiff, rest = take(3)
    (pair,) = take(1)
    frames_dev = blocks[0].shape[0]
    frames_all = number * frames_dev
    away = frames_all - 2 * frames_dev
    rows = plain.shape[0]
    states = gammas.shape[0] * LANES
    depth = rows // LANES
    _, window, core, _ = place()
    own_rows = pl.ds(pl.multiple_of(core * depth, depth), depth)
    tile = column_tile(width)
    if is_first:
        sums = [block[:, states:] for block in blocks[:2]] + [block[:, width:] for block in blocks[2:]]
        column_sums = jnp.dot(joined[...], jnp.concatenate(sums, axis=0), preferred_element_type=jnp.float32)
        turned = jnp.transpose(column_sums)
        line = turned[0:1] + turned[1:2] + turned[2:3]
        parts = [jnp.broadcast_to(part.astype(jnp.float32), (16, frames_all)).astype(jnp.bfloat16) for part in split3(line)]
        steps[:48, :] = jnp.concatenate(parts, axis=0)
        if away:
            steps[48:, :] = outer[...]
        step_matrix = steps
    else:
        step_matrix = outer
    for j in range(0, width, tile):
        local = [block[:, low_end + j : low_end + j + tile] for block in blocks[:2]]
        others = [block[:, j : j + tile] for block in blocks[2:]]
        member = jnp.concatenate(local + others, axis=0)
        product = jnp.dot(step_matrix[...], member, preferred_element_type=jnp.float32)
        mult_row = (product[0:1] + product[16:17] + product[32:33]) * 0.5
        for i in range(tile // LANES):
            mult_out[j // LANES + i : j // LANES + i + 1, :] = mult_row[:, i * LANES : (i + 1) * LANES]
        if away:
            pair[:away, j : j + tile] = product[48:].astype(jnp.bfloat16)
            pair[away:, j : j + tile] = jnp.concatenate(others, axis=0)
    stiff[...] = mult_out[...] / (gammas[low_end // LANES : high_end // LANES, :] * (1.0 / states))
    if is_first:
        own = pl.ds(pl.multiple_of(core * rows, rows), rows)
        if away:
            left[:, :away] = jnp.transpose(pair[away:, own])
            left[:, away:] = jnp.transpose(pair[:away, own])
        spread(stiff[own_rows, :], column)
        plain[...] = jnp.zeros_like(plain)
    else:
        plain[...] = plain_in[...]

    if is_last:
        mult_own = (mult_out if is_first else earlier_mult)[own_rows, :]

        half = depth // 2

        def half_for(target, block):
            first = lax.rem(target // (sent.shape[0] // number), 2) == 0
            return jnp.where(first, block[:half], block[half:])

        def put_mult(target):
            sent[target, :half] = half_for(target, mult_own)

        each(sent.shape[0], put_mult)
    for low in range(0, width, tile):
        columns = slice(low, low + tile)
        product = jnp.dot(left[...], pair[:, columns], preferred_element_type=jnp.float32) if away else None

        def counts_of(here):
            counts = counts_in[here, columns]
            if away:
                counts = counts + product[here]
            counts_out[here, columns] = counts
            return counts

        stiff_rows = [stiff[i : i + 1, :] for i in range(low // LANES, (low + tile) // LANES)]
        add_tile(counts_of, column, stiff_rows, plain)

    if is_last:
        own_stiff_ref = stiff if is_first else earlier_stiff
        new = own_stiff_ref[own_rows, :] * gathered(plain)
        stiff_refs = [stiff] if is_first else [earlier_stiff, stiff]
        counts_refs = [counts_out] if is_first else [earlier_counts, counts_out]
        whole = mult_own * 2.0
        rest[...] = whole - new

        @pl.when(jnp.min(rest[...] / whole) < SAFE)
        def _():
            plain[...] = jnp.zeros_like(plain)
            for count, stiff_ref in zip(counts_refs, stiff_refs):
                add_weighted(count, stiff_ref, 0, column, plain)
            rest[...] = gathered(plain)

        odds = new / rest[...]
        terms = rest[...] * states
        windows = sent.shape[0] // number

        def put_rest(target):
            own_window = lax.rem(target, windows) == window
            sent[target, half:] = jnp.where(own_window, half_for(target, odds), half_for(target, terms))

        each(sent.shape[0], put_rest)


def merge_kernel(number, given, merged):
    windows = given.shape[0] // number
    half = given.shape[1] // 2
    states = number * 2 * half * LANES
    window = place()[1]
    own_window = lax.broadcasted_iota(jnp.int32, (windows, half, LANES), 0) == window
    for block in range(number):
        here = slice(block * half, (block + 1) * half)
        block_mult = given[block * windows : (block + 1) * windows, :half]
        others = given[block * windows : (block + 1) * windows, half:]
        part = 2.0 * block_mult / (1.0 + others)
        terms = jnp.where(own_window, part * states, others)
        total = jnp.sum(block_mult, axis=0)
        merged[0, here, :] = total / jnp.sum(terms, axis=0)
        merged[1, here, :] = jnp.sum(jnp.where(own_window, part * others, 0.0), axis=0)
        merged[2, here, :] = total


def second_kernel(bounds, *refs):
    number_chunks = len(bounds)
    merged, beside, gammas = refs[:3]
    mults = refs[3 : 3 + number_chunks]
    counts = refs[3 + number_chunks : 3 + 2 * number_chunks]
    sent, logs_out, state_counts, new_mult, stiff, column, plain, rest = refs[3 + 2 * number_chunks :]
    depth = logs_out.shape[1] // LANES
    half = depth // 2
    states = gammas.shape[0] * LANES
    number = gammas.shape[0] // depth
    _, _, core, own_chip = place()
    for block in range(number):
        here = pl.ds(pl.multiple_of(lax.rem(block + (number - 2 * own_chip), number) * depth, depth), depth)
        whole = []
        for i in range(3):
            mine = merged[i, block * half : (block + 1) * half, :]
            theirs = beside[i, block * half : (block + 1) * half, :]
            whole.append(
                jnp.concatenate([jnp.where(core == 0, mine, theirs), jnp.where(core == 0, theirs, mine)], axis=0)
            )
        stiff[here, :] = whole[0]
        new_mult[here, :] = whole[1]
        state_counts[block * depth : (block + 1) * depth, :] = whole[2]
    raw = stiff[...]
    weights = raw / jnp.sum(raw)
    stiff[...] = new_mult[...] / (gammas[...] * weights)
    own = pl.ds(pl.multiple_of(core * depth, depth), depth)
    weights_own = new_mult[own, :] / (stiff[own, :] * gammas[own, :])
    spread(stiff[own, :], column)
    plain[...] = jnp.zeros_like(plain)
    for (low_end, high_end), count in zip(bounds, counts):
        width = high_end - low_end
        for low in range(0, width, SPAN):
            span = min(SPAN, width - low)
            start = (low_end + low) // LANES
            block = min(ROWS, plain.shape[0])

            @pl.loop(0, plain.shape[0] // block)
            def _(step):
                for inner in range(0, block, BLOCK):
                    here = pl.ds(pl.multiple_of(step * block + inner, BLOCK), BLOCK)
                    stiff_col = column[here, :]
                    total = plain[here, :]
                    for i in range(span // LANES):
                        cell = count[here, low + i * LANES : low + (i + 1) * LANES]
                        total = total + cell / (stiff_col + stiff[start + i : start + i + 1, :])
                    plain[here, :] = total

    whole = mults[0][own, :] * 2.0
    new = stiff[own, :] * gathered(plain)
    rest[...] = whole - new

    @pl.when(jnp.min(rest[...] / whole) < SAFE)
    def _():
        plain[...] = jnp.zeros_like(plain)
        for (low_end, _), count in zip(bounds, counts):
            add_weighted(count, stiff, low_end // LANES, column, plain)
        rest[...] = gathered(plain)

    terms = rest[...] / weights_own
    window_total = sum(jnp.sum(mult[...]) for mult in mults)
    logs = jnp.log(new * states / window_total)
    for i in range(depth):
        logs_out[:, i * LANES : (i + 1) * LANES] = logs[i : i + 1, :]

    def put(target):
        sent[target] = terms

    each(sent.shape[0], put)


def last_kernel(given, state_counts, energy_out, raw_ref):
    depth = energy_out.shape[0] // LANES
    states = state_counts.shape[0] * LANES
    number = state_counts.shape[0] // depth
    windows = given.shape[0] // number
    for block in range(number):
        here = slice(block * depth, (block + 1) * depth)
        terms = jnp.sum(given[block * windows : (block + 1) * windows], axis=0)
        raw_ref[here, :] = state_counts[here, :] / terms
    total = jnp.sum(raw_ref[...])
    own = pl.ds(pl.multiple_of(place()[0] * depth, depth), depth)
    energy = -jnp.log(raw_ref[own, :] / total * states)
    for i in range(depth):
        energy_out[i * LANES : (i + 1) * LANES] = energy[i]


def spot(*shape, dtype=jnp.float32):
    return pltpu.VMEM(shape, dtype)


def keep(x):
    return pltpu.with_memory_space_constraint(x, pltpu.VMEM)


def everyone(block):
    return lax.all_to_all(block, ("frames", "win"), 0, 0, tiled=True)


def call(kernel, ins, outs, scratch=(), scalars=(), limit=16, aliases={}, space=pltpu.VMEM):
    smem = pl.BlockSpec(memory_space=pltpu.SMEM)
    vmem = pl.BlockSpec(memory_space=pltpu.VMEM)
    return pl.pallas_call(
        kernel,
        out_shape=tuple(outs),
        in_specs=[smem] * len(scalars) + [pl.BlockSpec(memory_space=space)] * len(ins),
        out_specs=(vmem,) * len(outs),
        scratch_shapes=list(scratch),
        input_output_aliases=aliases,
        compiler_params=pltpu.CompilerParams(vmem_limit_bytes=limit << 20),
    )(*scalars, *ins)


def estimate(memberships, lag_times, segment_ids, bias_codes):
    frames_dev, states = memberships.shape[1:]
    frames_all = segment_ids.shape[1]
    number = lax.axis_size("frames")
    windows = lax.axis_size("win")
    rows = states // number
    depth = rows // LANES
    group = 2 * rows
    bounds = chunk_bounds(states, group)
    near = 2 * frames_dev
    away = frames_all - near
    half = jnp.bfloat16
    codes = bias_codes.reshape(states // LANES, LANES)
    partner = [(i, i ^ 1) for i in range(number)]
    widths = [high - low for low, high in bounds]
    sizes = [widths[0] + LANES] + widths[1:]
    shapes = [spot(frames_dev, states + LANES, dtype=half)]
    for _ in range(1, number // 2):
        shapes += [spot(frames_dev, width, dtype=half) for width in sizes]
    whole, *parts = call(
        lambda *refs: prepare_kernel(group, *refs),
        [pltpu.with_memory_space_constraint(memberships, pltpu.HBM)],
        shapes,
        [spot(1, frames_dev, states), pltpu.SemaphoreType.DMA((PIECES,))],
        space=pltpu.HBM,
    )
    route = lambda step: [((i + step) % number, i) for i in range(number)]
    across = []
    for chip in range(1, number // 2):
        across.append([])
        for c in range(len(bounds)):
            across[-1].append(lax.ppermute(parts[(chip - 1) * len(bounds) + c], "frames", route(2 * chip)))
    beside = lax.ppermute(whole, "frames", partner)
    inner, outer, joined, gammas = call(
        lambda *refs: plan_kernel(number, group, *refs),
        [pltpu.with_memory_space_constraint(x, pltpu.HBM) for x in (segment_ids, codes)],
        [
            spot(near, near, dtype=half),
            spot(max(away, 8), frames_all, dtype=half),
            spot(frames_all, frames_all, dtype=half),
            spot(states // LANES, LANES),
        ],
        [
            spot(1, frames_all, dtype=jnp.int32),
            spot(states // LANES, LANES, dtype=jnp.int32),
            pltpu.SemaphoreType.DMA((2,)),
        ],
        scalars=[lag_times],
        space=pltpu.HBM,
    )
    counts = call(
        lambda *refs: near_kernel(bounds, *refs),
        [whole, beside, keep(inner)],
        [spot(rows, width) for width in widths],
        [spot(2 * near, states, dtype=half), spot(rows, 2 * near, dtype=half)],
    )
    counts = list(counts)
    mults = []
    state = [outer, joined] if away else [joined]
    for c, width in enumerate(widths):
        first, last = c == 0, c == len(bounds) - 1
        blocks = [whole, beside]
        for chunk in across:
            arrived = chunk[c]
            if c:
                arrived, state[0] = lax.optimization_barrier((arrived, state[0]))
            blocks += [arrived, lax.ppermute(arrived, "frames", partner)]
        outs = [spot(rows, width), spot(width // LANES, LANES)]
        sums = [spot(rows, LANES), spot(width // LANES, LANES)]
        scratch = []
        if last:
            outs += [spot(number * windows, depth, LANES)]
        else:
            outs += sums
        fixed = [spot(rows, LANES), spot(rows, 2 * max(away, 8), dtype=half), spot(48 + away, frames_all, dtype=half)]
        if first:
            if last:
                scratch += fixed
            else:
                outs += fixed
        if last:
            scratch += sums + [spot(depth, LANES)]
        scratch += [spot(2 * max(away, 8), width, dtype=half)]
        results = call(
            lambda *refs, c=c: counts_kernel(bounds, c, number, *refs),
            [keep(gammas), keep(counts[c])] + blocks + [keep(x) for x in state],
            outs,
            scratch,
        )
        counts[c] = results[0]
        mults.append(results[1])
        if not last:
            state = [results[2]] + list(results[4:7]) + [results[3], results[1], results[0]]
    given = everyone(results[2])
    (merged,) = call(lambda *refs: merge_kernel(number, *refs), [given], [spot(3, states // LANES // 2, LANES)])
    beside = lax.ppermute(merged, "frames", partner)
    sums = [spot(states // LANES, LANES)] * 2 + [spot(rows, LANES)] * 2 + [spot(depth, LANES)]
    sent, logs, state_counts = call(
        lambda *refs: second_kernel(bounds, *refs),
        [merged, beside, keep(gammas)] + [keep(x) for x in mults + counts],
        [
            spot(number * windows, depth, LANES),
            jax.ShapeDtypeStruct((1, rows), jnp.float32),
            spot(states // LANES, LANES),
        ],
        sums,
    )
    given = everyone(sent)
    (energy,) = call(
        last_kernel,
        [given, keep(state_counts)],
        [jax.ShapeDtypeStruct((rows,), jnp.float32)],
        [spot(states // LANES, LANES)],
    )
    return energy, logs


def solution(mesh):
    placed = (P("win", "frames", None), P("win"), P("win", None), P("win", None))
    return jax.shard_map(
        estimate,
        mesh=mesh,
        in_specs=placed,
        out_specs=(P("frames"), P("win", "frames")),
        check_vma=False,
    )
```

```python
import math

import jax
import jax.numpy as jnp
from jax import lax
from jax.experimental import pallas as pl
from jax.experimental.pallas import tpu as pltpu
from jax.sharding import PartitionSpec as P


LANES = 128
SAFE = 1.0 / 512.0
BLOCK = 64
ROWS = 256
SPAN = 2048
PIECES = 4

bias_unit = 1.0 / 128.0


def chunk_bounds(states, group):
    return [(0, group), (group, states)] if states > group else [(0, states)]


def granule(states, group):
    size = group
    for low, high in chunk_bounds(states, group):
        size = math.gcd(size, high - low)
    return size


def wrapped(place, states):
    return jnp.where(place >= states, place - states, place)


def split3(x):
    high = x.astype(jnp.bfloat16)
    rest = x - high.astype(jnp.float32)
    middle = rest.astype(jnp.bfloat16)
    low = (rest - middle.astype(jnp.float32)).astype(jnp.bfloat16)
    return high, middle, low


def gamma_of(codes):
    return jnp.exp(codes.astype(jnp.float32) * -bias_unit)


def spread(folded, column_ref):
    for i in range(folded.shape[0]):
        square = jnp.broadcast_to(folded[i : i + 1, :], (LANES, LANES))
        column_ref[i * LANES : (i + 1) * LANES, :] = jnp.transpose(square)


def gathered(partial_ref):
    rows = partial_ref.shape[0]
    return jnp.concatenate(
        [
            jnp.sum(jnp.transpose(partial_ref[i : i + LANES, :]), axis=0, keepdims=True)
            for i in range(0, rows, LANES)
        ],
        axis=0,
    )


def column_tile(width):
    for tile in (512, 256, 128):
        if width % tile == 0:
            return tile


def add_tile(counts_of, column, stiff_rows, plain_ref):
    rows = plain_ref.shape[0]
    for first in range(0, rows, BLOCK):
        here = slice(first, first + BLOCK)
        counts = counts_of(here)
        stiff_col = column[here, :]
        plain = plain_ref[here, :]
        for i, stiff_row in enumerate(stiff_rows):
            plain = plain + counts[:, i * LANES : (i + 1) * LANES] / (stiff_col + stiff_row)
        plain_ref[here, :] = plain


def add_weighted(count, stiff, first, column, partial):
    @pl.loop(0, count.shape[1] // LANES)
    def _(step):
        columns = pl.ds(pl.multiple_of(step * LANES, LANES), LANES)
        stiff_row = stiff[pl.ds(first + step, 1), :]
        partial[...] += count[:, columns] / (column[...] + stiff_row) * stiff_row


def each(number, put):
    if number <= 64:
        for target in range(number):
            put(target)
    else:
        pl.loop(0, number)(put)


def place():
    position = lax.axis_index("frames")
    return position, lax.axis_index("win"), position % 2, position // 2


def fetched(sources, targets, sem):
    copies = [pltpu.make_async_copy(a, b, sem.at[i]) for i, (a, b) in enumerate(zip(sources, targets))]
    for copy in copies:
        copy.start()
    for copy in copies:
        copy.wait()


def prepare_kernel(group, given, *outs):
    member, sem = outs[-2:]
    whole, parts = outs[0], outs[1:-2]
    height = given.shape[1] // PIECES
    pieces = [pl.ds(i * height, height) for i in range(PIECES)]
    fetched([given.at[:, piece, :] for piece in pieces], [member.at[:, piece, :] for piece in pieces], sem)
    frames_dev, states = member.shape[1:]
    bounds = chunk_bounds(states, group)
    size = granule(states, group)
    own_chip = place()[3]
    total = jnp.zeros((frames_dev, LANES), jnp.float32)
    for j in range(0, states, size):
        source = pl.multiple_of(wrapped(own_chip * group + j, states), size)
        block = member[0, :, pl.ds(source, size)].astype(jnp.bfloat16)
        whole[:, j : j + size] = block
        wide = block.astype(jnp.float32)
        for i in range(0, size, LANES):
            total = total + wide[:, i : i + LANES]
    sums = jnp.broadcast_to(jnp.sum(total, axis=1, keepdims=True), (frames_dev, LANES))
    high, middle, low = split3(sums)
    lane = lax.broadcasted_iota(jnp.int32, sums.shape, 1)
    none = jnp.zeros_like(sums)
    packed = jnp.where(lane == 0, high.astype(jnp.float32), none)
    packed = jnp.where(lane == 1, middle.astype(jnp.float32), packed)
    packed = jnp.where(lane == 2, low.astype(jnp.float32), packed).astype(jnp.bfloat16)
    whole[:, states:] = packed
    for chip in range(1, states // group):
        base = (own_chip - chip) * group
        base = jnp.where(base < 0, base + states, base)
        for c, (low_end, high_end) in enumerate(bounds):
            part = parts[(chip - 1) * len(bounds) + c]
            for j in range(low_end, high_end, size):
                source = pl.multiple_of(wrapped(base + j, states), size)
                part[:, j - low_end : j - low_end + size] = member[0, :, pl.ds(source, size)].astype(jnp.bfloat16)
            if c == 0:
                part[:, high_end:] = packed


def plan_kernel(number, group, lag, segments_in, codes_in, inner, outer, joined, gammas, segments, codes, sem):
    fetched([segments_in, codes_in], [segments, codes], sem)
    frames_all = segments.shape[1]
    frames_dev = frames_all // number
    near = 2 * frames_dev
    _, _, core, own_chip = place()
    lag_time = lag[0]
    grid = (frames_all, frames_all)
    row = lax.broadcasted_iota(jnp.int32, grid, 0)
    frame = row
    for i in range(number):
        owner = lax.rem(own_chip + i // 2, number // 2) * 2 + (core if i % 2 == 0 else 1 - core)
        inside = (row >= i * frames_dev) & (row < (i + 1) * frames_dev)
        frame = jnp.where(inside, row + (owner - i) * frames_dev, frame)
    frame = frame.astype(jnp.float32)
    seg_row = jnp.broadcast_to(segments[...].astype(jnp.float32), grid)
    col = lax.broadcasted_iota(jnp.int32, grid, 1).astype(jnp.float32)
    seg = jnp.sum(jnp.where(frame == col, seg_row, 0.0), axis=1, keepdims=True)
    seg_from = jnp.broadcast_to(seg, grid)
    seg_to = jnp.transpose(seg_from)
    frame_to = jnp.transpose(frame)
    ahead = frame_to - frame
    same = seg_from == seg_to
    lag_float = lag_time.astype(jnp.float32)
    forward = same & (ahead == lag_float)
    backward = same & (ahead == -lag_float)
    joined[...] = jnp.where(forward | backward, 1.0, 0.0).astype(jnp.bfloat16)
    forward = jnp.where(forward, 1.0, 0.0)
    inner[...] = forward[:near, :near].astype(jnp.bfloat16)
    if number > 2:
        below = frame < (own_chip * near).astype(jnp.float32)
        touching = jnp.where(below, forward, jnp.where(backward, 1.0, 0.0))
        outer[...] = touching[near:, :].astype(jnp.bfloat16)
    size = granule(codes.shape[0] * LANES, group) // LANES
    for i in range(0, codes.shape[0], size):
        start = wrapped(own_chip * (group // LANES) + i, codes.shape[0])
        gammas[i : i + size, :] = gamma_of(codes[pl.ds(pl.multiple_of(start, size), size), :])


def near_kernel(bounds, whole, beside, inner, *refs):
    counts = refs[: len(bounds)]
    pair, left = refs[len(bounds) :]
    frames_dev = whole.shape[0]
    near = 2 * frames_dev
    rows = left.shape[0]
    states = pair.shape[1]
    own = pl.ds(pl.multiple_of(place()[2] * rows, rows), rows)
    pair[near : near + frames_dev, :] = whole[:, :states]
    pair[near + frames_dev :, :] = beside[:, :states]
    pair[:near, :] = jnp.dot(inner[...], pair[near:, :], preferred_element_type=jnp.float32).astype(jnp.bfloat16)
    left[:, :near] = jnp.transpose(pair[near:, own])
    left[:, near:] = jnp.transpose(pair[:near, own])
    for (low_end, high_end), count in zip(bounds, counts):
        tile = column_tile(high_end - low_end)

        @pl.loop(0, (high_end - low_end) // tile)
        def _(step):
            here = pl.ds(pl.multiple_of(step * tile, tile), tile)
            there = pl.ds(pl.multiple_of(low_end + step * tile, tile), tile)
            count[:, here] = jnp.dot(left[...], pair[:, there], preferred_element_type=jnp.float32)


def counts_kernel(bounds, which, number, *refs):
    low_end, high_end = bounds[which]
    width = high_end - low_end
    is_first, is_last = which == 0, which == len(bounds) - 1
    refs = list(refs)
    take = lambda k: [refs.pop(0) for _ in range(k)]
    gammas, counts_in = take(2)
    blocks = take(number)
    far = number > 2
    if is_first:
        outer, joined = take(2) if far else take(1) * 2
    else:
        plain_in, column, left, outer, earlier_stiff, earlier_mult, earlier_counts = take(7)
    counts_out, mult_out = take(2)
    if is_last:
        (sent,) = take(1)
    else:
        plain, stiff = take(2)
    if is_first:
        column, left, steps = take(3)
    if is_last:
        plain, stiff, rest = take(3)
    (pair,) = take(1)
    frames_dev = blocks[0].shape[0]
    frames_all = number * frames_dev
    away = frames_all - 2 * frames_dev
    rows = plain.shape[0]
    states = gammas.shape[0] * LANES
    depth = rows // LANES
    _, window, core, _ = place()
    own_rows = pl.ds(pl.multiple_of(core * depth, depth), depth)
    tile = column_tile(width)
    if is_first:
        sums = [block[:, states:] for block in blocks[:2]] + [block[:, width:] for block in blocks[2:]]
        column_sums = jnp.dot(joined[...], jnp.concatenate(sums, axis=0), preferred_element_type=jnp.float32)
        turned = jnp.transpose(column_sums)
        line = turned[0:1] + turned[1:2] + turned[2:3]
        parts = [jnp.broadcast_to(part.astype(jnp.float32), (16, frames_all)).astype(jnp.bfloat16) for part in split3(line)]
        steps[:48, :] = jnp.concatenate(parts, axis=0)
        if away:
            steps[48:, :] = outer[...]
        step_matrix = steps
    else:
        step_matrix = outer
    for j in range(0, width, tile):
        local = [block[:, low_end + j : low_end + j + tile] for block in blocks[:2]]
        others = [block[:, j : j + tile] for block in blocks[2:]]
        member = jnp.concatenate(local + others, axis=0)
        product = jnp.dot(step_matrix[...], member, preferred_element_type=jnp.float32)
        mult_row = (product[0:1] + product[16:17] + product[32:33]) * 0.5
        for i in range(tile // LANES):
            mult_out[j // LANES + i : j // LANES + i + 1, :] = mult_row[:, i * LANES : (i + 1) * LANES]
        if away:
            pair[:away, j : j + tile] = product[48:].astype(jnp.bfloat16)
            pair[away:, j : j + tile] = jnp.concatenate(others, axis=0)
    stiff[...] = mult_out[...] / (gammas[low_end // LANES : high_end // LANES, :] * (1.0 / states))
    if is_first:
        own = pl.ds(pl.multiple_of(core * rows, rows), rows)
        if away:
            left[:, :away] = jnp.transpose(pair[away:, own])
            left[:, away:] = jnp.transpose(pair[:away, own])
        spread(stiff[own_rows, :], column)
        plain[...] = jnp.zeros_like(plain)
    else:
        plain[...] = plain_in[...]

    if is_last:
        mult_own = (mult_out if is_first else earlier_mult)[own_rows, :]

        half = depth // 2

        def half_for(target, block):
            first = lax.rem(target // (sent.shape[0] // number), 2) == 0
            return jnp.where(first, block[:half], block[half:])

        def put_mult(target):
            sent[target, :half] = half_for(target, mult_own)

        each(sent.shape[0], put_mult)
    for low in range(0, width, tile):
        columns = slice(low, low + tile)
        product = jnp.dot(left[...], pair[:, columns], preferred_element_type=jnp.float32) if away else None

        def counts_of(here):
            counts = counts_in[here, columns]
            if away:
                counts = counts + product[here]
            counts_out[here, columns] = counts
            return counts

        stiff_rows = [stiff[i : i + 1, :] for i in range(low // LANES, (low + tile) // LANES)]
        add_tile(counts_of, column, stiff_rows, plain)

    if is_last:
        own_stiff_ref = stiff if is_first else earlier_stiff
        new = own_stiff_ref[own_rows, :] * gathered(plain)
        stiff_refs = [stiff] if is_first else [earlier_stiff, stiff]
        counts_refs = [counts_out] if is_first else [earlier_counts, counts_out]
        whole = mult_own * 2.0
        rest[...] = whole - new

        @pl.when(jnp.min(rest[...] / whole) < SAFE)
        def _():
            plain[...] = jnp.zeros_like(plain)
            for count, stiff_ref in zip(counts_refs, stiff_refs):
                add_weighted(count, stiff_ref, 0, column, plain)
            rest[...] = gathered(plain)

        odds = new / rest[...]
        terms = rest[...] * states
        windows = sent.shape[0] // number

        def put_rest(target):
            own_window = lax.rem(target, windows) == window
            sent[target, half:] = jnp.where(own_window, half_for(target, odds), half_for(target, terms))

        each(sent.shape[0], put_rest)


def merge_kernel(number, given, merged):
    windows = given.shape[0] // number
    half = given.shape[1] // 2
    states = number * 2 * half * LANES
    window = place()[1]
    own_window = lax.broadcasted_iota(jnp.int32, (windows, half, LANES), 0) == window
    for block in range(number):
        here = slice(block * half, (block + 1) * half)
        block_mult = given[block * windows : (block + 1) * windows, :half]
        others = given[block * windows : (block + 1) * windows, half:]
        part = 2.0 * block_mult / (1.0 + others)
        terms = jnp.where(own_window, part * states, others)
        total = jnp.sum(block_mult, axis=0)
        merged[0, here, :] = total / jnp.sum(terms, axis=0)
        merged[1, here, :] = jnp.sum(jnp.where(own_window, part * others, 0.0), axis=0)
        merged[2, here, :] = total


def second_kernel(bounds, *refs):
    number_chunks = len(bounds)
    merged, beside, gammas = refs[:3]
    mults = refs[3 : 3 + number_chunks]
    counts = refs[3 + number_chunks : 3 + 2 * number_chunks]
    sent, logs_out, state_counts, new_mult, stiff, column, plain, rest = refs[3 + 2 * number_chunks :]
    depth = logs_out.shape[0]
    half = depth // 2
    states = gammas.shape[0] * LANES
    number = gammas.shape[0] // depth
    _, _, core, own_chip = place()
    for block in range(number):
        here = pl.ds(pl.multiple_of(lax.rem(block + (number - 2 * own_chip), number) * depth, depth), depth)
        whole = []
        for i in range(3):
            mine = merged[i, block * half : (block + 1) * half, :]
            theirs = beside[i, block * half : (block + 1) * half, :]
            whole.append(
                jnp.concatenate([jnp.where(core == 0, mine, theirs), jnp.where(core == 0, theirs, mine)], axis=0)
            )
        stiff[here, :] = whole[0]
        new_mult[here, :] = whole[1]
        state_counts[block * depth : (block + 1) * depth, :] = whole[2]
    raw = stiff[...]
    weights = raw / jnp.sum(raw)
    stiff[...] = new_mult[...] / (gammas[...] * weights)
    own = pl.ds(pl.multiple_of(core * depth, depth), depth)
    weights_own = new_mult[own, :] / (stiff[own, :] * gammas[own, :])
    spread(stiff[own, :], column)
    plain[...] = jnp.zeros_like(plain)
    for (low_end, high_end), count in zip(bounds, counts):
        width = high_end - low_end
        for low in range(0, width, SPAN):
            span = min(SPAN, width - low)
            start = (low_end + low) // LANES
            block = min(ROWS, plain.shape[0])

            @pl.loop(0, plain.shape[0] // block)
            def _(step):
                for inner in range(0, block, BLOCK):
                    here = pl.ds(pl.multiple_of(step * block + inner, BLOCK), BLOCK)
                    stiff_col = column[here, :]
                    total = plain[here, :]
                    for i in range(span // LANES):
                        cell = count[here, low + i * LANES : low + (i + 1) * LANES]
                        total = total + cell / (stiff_col + stiff[start + i : start + i + 1, :])
                    plain[here, :] = total

    whole = mults[0][own, :] * 2.0
    new = stiff[own, :] * gathered(plain)
    rest[...] = whole - new

    @pl.when(jnp.min(rest[...] / whole) < SAFE)
    def _():
        plain[...] = jnp.zeros_like(plain)
        for (low_end, _), count in zip(bounds, counts):
            add_weighted(count, stiff, low_end // LANES, column, plain)
        rest[...] = gathered(plain)

    terms = rest[...] / weights_own
    window_total = sum(jnp.sum(mult[...]) for mult in mults)
    logs_out[...] = jnp.log(new * states / window_total)

    def put(target):
        sent[target] = terms

    each(sent.shape[0], put)


def last_kernel(given, state_counts, logs, energy_out, logs_out, raw_ref):
    for i in range(logs.shape[0]):
        logs_out[:, i * LANES : (i + 1) * LANES] = logs[i : i + 1, :]
    depth = energy_out.shape[0] // LANES
    states = state_counts.shape[0] * LANES
    number = state_counts.shape[0] // depth
    windows = given.shape[0] // number
    for block in range(number):
        here = slice(block * depth, (block + 1) * depth)
        terms = jnp.sum(given[block * windows : (block + 1) * windows], axis=0)
        raw_ref[here, :] = state_counts[here, :] / terms
    total = jnp.sum(raw_ref[...])
    own = pl.ds(pl.multiple_of(place()[0] * depth, depth), depth)
    energy = -jnp.log(raw_ref[own, :] / total * states)
    for i in range(depth):
        energy_out[i * LANES : (i + 1) * LANES] = energy[i]


def spot(*shape, dtype=jnp.float32):
    return pltpu.VMEM(shape, dtype)


def keep(x):
    return pltpu.with_memory_space_constraint(x, pltpu.VMEM)


def everyone(block):
    return lax.all_to_all(block, ("frames", "win"), 0, 0, tiled=True)


def call(kernel, ins, outs, scratch=(), scalars=(), limit=16, aliases={}, space=pltpu.VMEM):
    smem = pl.BlockSpec(memory_space=pltpu.SMEM)
    vmem = pl.BlockSpec(memory_space=pltpu.VMEM)
    return pl.pallas_call(
        kernel,
        out_shape=tuple(outs),
        in_specs=[smem] * len(scalars) + [pl.BlockSpec(memory_space=space)] * len(ins),
        out_specs=(vmem,) * len(outs),
        scratch_shapes=list(scratch),
        input_output_aliases=aliases,
        compiler_params=pltpu.CompilerParams(vmem_limit_bytes=limit << 20),
    )(*scalars, *ins)


def estimate(memberships, lag_times, segment_ids, bias_codes):
    frames_dev, states = memberships.shape[1:]
    frames_all = segment_ids.shape[1]
    number = lax.axis_size("frames")
    windows = lax.axis_size("win")
    rows = states // number
    depth = rows // LANES
    group = 2 * rows
    bounds = chunk_bounds(states, group)
    near = 2 * frames_dev
    away = frames_all - near
    half = jnp.bfloat16
    codes = bias_codes.reshape(states // LANES, LANES)
    partner = [(i, i ^ 1) for i in range(number)]
    widths = [high - low for low, high in bounds]
    sizes = [widths[0] + LANES] + widths[1:]
    shapes = [spot(frames_dev, states + LANES, dtype=half)]
    for _ in range(1, number // 2):
        shapes += [spot(frames_dev, width, dtype=half) for width in sizes]
    whole, *parts = call(
        lambda *refs: prepare_kernel(group, *refs),
        [pltpu.with_memory_space_constraint(memberships, pltpu.HBM)],
        shapes,
        [spot(1, frames_dev, states), pltpu.SemaphoreType.DMA((PIECES,))],
        space=pltpu.HBM,
    )
    route = lambda step: [((i + step) % number, i) for i in range(number)]
    across = []
    for chip in range(1, number // 2):
        across.append([])
        for c in range(len(bounds)):
            across[-1].append(lax.ppermute(parts[(chip - 1) * len(bounds) + c], "frames", route(2 * chip)))
    beside = lax.ppermute(whole, "frames", partner)
    inner, outer, joined, gammas = call(
        lambda *refs: plan_kernel(number, group, *refs),
        [pltpu.with_memory_space_constraint(x, pltpu.HBM) for x in (segment_ids, codes)],
        [
            spot(near, near, dtype=half),
            spot(max(away, 8), frames_all, dtype=half),
            spot(frames_all, frames_all, dtype=half),
            spot(states // LANES, LANES),
        ],
        [
            spot(1, frames_all, dtype=jnp.int32),
            spot(states // LANES, LANES, dtype=jnp.int32),
            pltpu.SemaphoreType.DMA((2,)),
        ],
        scalars=[lag_times],
        space=pltpu.HBM,
    )
    counts = call(
        lambda *refs: near_kernel(bounds, *refs),
        [whole, beside, keep(inner)],
        [spot(rows, width) for width in widths],
        [spot(2 * near, states, dtype=half), spot(rows, 2 * near, dtype=half)],
    )
    counts = list(counts)
    mults = []
    state = [outer, joined] if away else [joined]
    for c, width in enumerate(widths):
        first, last = c == 0, c == len(bounds) - 1
        blocks = [whole, beside]
        for chunk in across:
            arrived = chunk[c]
            if c:
                arrived, state[0] = lax.optimization_barrier((arrived, state[0]))
            blocks += [arrived, lax.ppermute(arrived, "frames", partner)]
        outs = [spot(rows, width), spot(width // LANES, LANES)]
        sums = [spot(rows, LANES), spot(width // LANES, LANES)]
        scratch = []
        if last:
            outs += [spot(number * windows, depth, LANES)]
        else:
            outs += sums
        fixed = [spot(rows, LANES), spot(rows, 2 * max(away, 8), dtype=half), spot(48 + away, frames_all, dtype=half)]
        if first:
            if last:
                scratch += fixed
            else:
                outs += fixed
        if last:
            scratch += sums + [spot(depth, LANES)]
        scratch += [spot(2 * max(away, 8), width, dtype=half)]
        results = call(
            lambda *refs, c=c: counts_kernel(bounds, c, number, *refs),
            [keep(gammas), keep(counts[c])] + blocks + [keep(x) for x in state],
            outs,
            scratch,
        )
        counts[c] = results[0]
        mults.append(results[1])
        if not last:
            state = [results[2]] + list(results[4:7]) + [results[3], results[1], results[0]]
    given = everyone(results[2])
    (merged,) = call(lambda *refs: merge_kernel(number, *refs), [given], [spot(3, states // LANES // 2, LANES)])
    beside = lax.ppermute(merged, "frames", partner)
    sums = [spot(states // LANES, LANES)] * 2 + [spot(rows, LANES)] * 2 + [spot(depth, LANES)]
    sent, logs, state_counts = call(
        lambda *refs: second_kernel(bounds, *refs),
        [merged, beside, keep(gammas)] + [keep(x) for x in mults + counts],
        [
            spot(number * windows, depth, LANES),
            spot(depth, LANES),
            spot(states // LANES, LANES),
        ],
        sums,
    )
    given = everyone(sent)
    energy, logs = call(
        last_kernel,
        [given, keep(state_counts), keep(logs)],
        [jax.ShapeDtypeStruct((rows,), jnp.float32), jax.ShapeDtypeStruct((1, rows), jnp.float32)],
        [spot(states // LANES, LANES)],
    )
    return energy, logs


def solution(mesh):
    placed = (P("win", "frames", None), P("win"), P("win", None), P("win", None))
    return jax.shard_map(
        estimate,
        mesh=mesh,
        in_specs=placed,
        out_specs=(P("frames"), P("win", "frames")),
        check_vma=False,
    )
```
